128 devices in a mesh: gx: 4 (over y), gy: 32 (over z, x, core).
Axes of the slice: x: 4, y: 4, z: 4, core: 2. Of those that a mesh axis runs over, the one named last changes fastest.
Arguments:
- patches: bfloat16 [256, 4096, 256], P(('gx', 'gy')), may hold values from -6 to 6
- start_frames: float32 [256, 256, 256], P(('gx', 'gy')), may hold values from -6 to 6
- pair_ends: int32 [1024, 2], P('gx'), may hold values from 0 to 255, as said below
- margin_blocks: int32 [1024, 2, 4], P('gx'), may hold values from 0 to 31, as said below
Outputs:
- aligned: bfloat16 [256, 4096, 256], P(('gx', 'gy'))
- final_frames: float32 [256, 256, 256], P(('gx', 'gy'))
- frame_total: float32 [256, 256], replicated
The draws below stay inside these ranges and needn't reach their ends.
Inputs may be any that keep to these rules, and one draw needn't show every extreme that they name: `pair_ends`: both ends of a pair lie in the owner's group of 64 patches (patches of the devices with the owner's gx index), on distinct patches; at most 1 ends of one owner's pairs lie on any one device, and ends on one device are of distinct patches; some device holds exactly 1 of some owner's ends. Every patch is an end of some pair. Patch p lives on device p // 2, devices counted with gx slowest. Patch degrees are uneven. `margin_blocks`: the 4 blocks of one end are distinct.
All inputs are finite; a program needn't handle non-finite values.
Results may differ from the reference program's by a relative error of at most 0.012.
The reference program's roundings to bfloat16 on the way count: a program that leaves them out, or rounds other values in their place, can miss the bound.
Values may be sent and summed in bfloat16 or wider, within the bound.
No kernel may reach another device: no remote copies, remote signals or barrier semaphores. Data moves between devices by JAX's collectives and lax.ppermute only.
A program may use at most 128 MiB of HBM per device.

```python
import jax
import jax.numpy as jnp
from jax import lax

D = 256
P_DEV = 2
ROWS = 4096
BLOCK = 128
OVB = 4
PAIRS_DEV = 8
SWEEPS = 2
NS_STEPS = 5
GROUP_DEVICES = 32
GROUP_PATCHES = 64
PATCHES = 256
PAIRS = 1024
CAP = 1


def draw_pair_ends(key, part):
    owner_count = PAIRS // PAIRS_DEV
    ends_count = 2 * PAIRS_DEV
    slot_count = GROUP_DEVICES * CAP
    weight_key, owner_key = jax.random.split(key)
    weights = jax.random.randint(weight_key, (owner_count // GROUP_DEVICES, GROUP_DEVICES), 1, 9)

    def one_owner(single_key, owner):
        group = owner // GROUP_DEVICES
        local_owner = owner % GROUP_DEVICES
        score_key, bit_key = jax.random.split(single_key)
        slot_device = jnp.arange(slot_count) // CAP
        slot_within = jnp.arange(slot_count) % CAP
        device_numbers = jnp.arange(GROUP_DEVICES)
        cover_index = jnp.arange(P_DEV)
        cover_device = (local_owner + 1 + cover_index) % GROUP_DEVICES
        cover_match = device_numbers[:, None] == cover_device[None, :]
        has_cover = jnp.sum(cover_match.astype(jnp.int32), axis=1) > 0
        cover_patch = jnp.sum(cover_match.astype(jnp.int32) * cover_index[None, :], axis=1)
        forced = has_cover[slot_device] & (slot_within == 0)
        raw_score = jax.random.randint(score_key, (slot_count,), 0, 65536) * weights[group][slot_device]
        raw_score = jnp.where(forced, 1000000, raw_score)
        scores = raw_score * slot_count + jnp.arange(slot_count)
        chosen = lax.top_k(scores, ends_count)[1]
        device = chosen // CAP
        positions = jnp.arange(ends_count)
        same_device = device[:, None] == device[None, :]
        earlier = positions[None, :] < positions[:, None]
        occurrence = jnp.sum(same_device & earlier, axis=1)
        offsets = jax.random.randint(bit_key, (GROUP_DEVICES,), 0, P_DEV)
        offsets = jnp.where(has_cover, cover_patch, offsets)
        local_patch = (offsets[device] + occurrence) % P_DEV
        return group * GROUP_PATCHES + device * P_DEV + local_patch
    owner_keys = jax.random.split(owner_key, owner_count)
    result = jax.vmap(one_owner)(owner_keys, jnp.arange(owner_count))
    return result.reshape(PAIRS, 2).astype(jnp.int32)


def draw_margin_blocks(key, part):
    block_count = ROWS // BLOCK
    scores = jax.random.randint(key, (PAIRS, 2, block_count), 0, 65536) * block_count + jnp.arange(block_count)
    return lax.top_k(scores, OVB)[1].astype(jnp.int32)


def levels(key, shape, cuts, low, high):
    level, own = 1.0, jax.random.fold_in(key, 6)
    for position, shards_of in cuts:
        heights = jnp.exp(jax.random.uniform(jax.random.fold_in(own, position), (shards_of,), jnp.float32, low / len(cuts), high / len(cuts)))
        level = level * jnp.repeat(heights, shape[position] // shards_of).reshape([-1 if axis == position else 1 for axis in range(len(shape))])
    return level


def normal_values(key, extent, deviation, bound, shards=(), kind=jnp.bfloat16):
    values = deviation * jax.random.normal(key, extent, jnp.float32)
    if shards:
        values = values * levels(key, extent, shards, -0.22, 0.18)
    return jnp.clip(values, -bound, bound).astype(kind)


def setup_inputs(seed: int = 0) -> dict:
    keys = jax.random.split(jax.random.key(seed), 5)
    return {
        "patches": normal_values(keys[0], (PATCHES, ROWS, D), 1.0, 6.0, ((0, 128),)),
        "start_frames": normal_values(keys[1], (PATCHES, D, D), 1.0, 6.0, ((0, 128),), jnp.float32),
        "pair_ends": draw_pair_ends(jax.random.fold_in(keys[4], 71), 0),
        "margin_blocks": draw_margin_blocks(jax.random.fold_in(keys[4], 71), 0),
    }


coef_first = 3.4445
coef_second = -4.775
coef_third = 2.0315

def newton_schulz(matrix):
    scaling = lax.rsqrt(lax.optimization_barrier(jnp.sum(matrix * matrix, axis=(-2, -1), keepdims=True)) + 1e-06)
    matrix = matrix * scaling
    for repeat_index in range(NS_STEPS):
        square = jnp.einsum('...ij,...kj->...ik', matrix, matrix, precision=lax.Precision.HIGHEST)
        polynom = coef_second * square + coef_third * jnp.einsum('...ij,...jk->...ik', square, square, precision=lax.Precision.HIGHEST)
        matrix = coef_first * matrix + jnp.einsum('...ij,...jk->...ik', polynom, matrix, precision=lax.Precision.HIGHEST)
    return matrix

def reference(patches, start_frames, pair_ends, margin_blocks):
    flat_rows = patches.reshape(PATCHES * ROWS, D)
    offsets = jnp.arange(BLOCK).astype(jnp.int32)
    row_index = (pair_ends[:, :, None, None] * ROWS + margin_blocks[:, :, :, None] * BLOCK + offsets[None, None, None, :]).astype(jnp.int32)
    row_index = row_index.reshape(PAIRS // PAIRS_DEV, PAIRS_DEV, 2 * OVB * BLOCK)

    def pair_rotations(indices):
        gathered = jnp.take(flat_rows, indices.reshape(-1), axis=0).reshape(PAIRS_DEV, 2, OVB * BLOCK, D).astype(jnp.float32)
        gram = jnp.einsum('pri,prj->pij', gathered[:, 1], gathered[:, 0], precision=lax.Precision.HIGHEST)
        return newton_schulz(gram)
    rotation = lax.map(pair_rotations, row_index).reshape(PAIRS, D, D)
    q_ends = jnp.stack([jnp.swapaxes(rotation, 1, 2), rotation], axis=1).reshape(2 * PAIRS, D, D)
    end_ids = pair_ends.reshape(-1).astype(jnp.int32)
    partner_ids = pair_ends[:, ::-1].reshape(-1).astype(jnp.int32)
    frames = newton_schulz(start_frames)
    for iteration in range(SWEEPS):
        frames_low = frames.astype(jnp.bfloat16)
        partner = jnp.take(frames_low, partner_ids, axis=0).astype(jnp.float32)
        estimate = jnp.einsum('eij,ejk->eik', q_ends, partner, precision=lax.Precision.HIGHEST)
        summed = jax.ops.segment_sum(estimate, end_ids, num_segments=PATCHES)
        frames = newton_schulz(frames + summed)
    total_frame = lax.optimization_barrier(jnp.sum(frames, axis=0))
    gauge = newton_schulz(total_frame)
    final_frames = jnp.einsum('pij,kj->pik', frames, gauge, precision=lax.Precision.HIGHEST)
    frames_low = final_frames.astype(jnp.bfloat16)

    def rotate_patch(operands):
        rows, frame = operands
        return jnp.dot(rows, frame, preferred_element_type=jnp.float32).astype(jnp.bfloat16)
    aligned = lax.map(rotate_patch, (patches, frames_low))
    return (aligned, final_frames, total_frame)
```

```python
import functools

import jax
import jax.numpy as jnp
import numpy as np
from jax import lax
from jax.experimental import pallas as pl
from jax.experimental.pallas import tpu as pltpu
from jax.sharding import Mesh
from jax.sharding import PartitionSpec as P

BLOCK = 128
OVB = 4
D = 256
SWEEPS = 2
NS_STEPS = 5
PER = 2
DEVS = 32
BATCH = 4
GY = ("gy_0", "gy_1", "gy_2")
GX_GY = ("gx", "gy_0", "gy_1", "gy_2")
F32, BF16 = jnp.float32, jnp.bfloat16

coef_first = 3.4445
coef_second = -4.775
coef_third = 2.0315

OFFS = (
    ((0, 0), (1, 0), (2, 0), (0, 1), (0, 3), (0, 2)),
    ((0, 0), (0, 1), (0, 2), (1, 0), (3, 0), (2, 0)),
)
CROSS = (1, 2, 3)
OWN = len(OFFS[0])
SLOTS = OWN + len(CROSS)
MAX_PAIRS = -(-(SLOTS * DEVS // 2) // BATCH) * BATCH


def device_at(z, x, c):
    return (z % 4) * 8 + (x % 4) * 2 + c % 2


def place_of(m):
    return m // 8, (m // 2) % 4, m % 2


def step_perm(steps):
    perm = []
    for m in range(DEVS):
        z, x, c = place_of(m)
        dz, dx = steps[c]
        perm.append((m, device_at(z + dz, x + dx, c)))
    return perm


def flip(step):
    return (step, (step[1], step[0]))


UP, RIGHT, LEFT = flip((1, 0)), flip((0, 1)), flip((0, -1))
SIBLING = [(m, m ^ 1) for m in range(DEVS)]


@functools.cache
def sources():
    same = []
    for m in range(DEVS):
        z, x, c = place_of(m)
        same.append([device_at(z - dz, x - dx, c) for dz, dx in OFFS[c]])
    return [same[m] + [same[m ^ 1][k] for k in CROSS] for m in range(DEVS)]


@functools.cache
def meeting_table():
    found = {}
    src = sources()
    for m in range(DEVS):
        for i in range(SLOTS):
            for j in range(SLOTS):
                if src[m][i] != src[m][j]:
                    found.setdefault((src[m][i], src[m][j]), []).append((m, i, j))
    load = [0] * DEVS
    table = np.zeros((DEVS, DEVS), np.int32)
    order = sorted(
        ((a, b) for a in range(DEVS) for b in range(a + 1, DEVS)),
        key=lambda ab: (len({t[0] for t in found[ab]}), ab),
    )
    for a, b in order:
        m, i, j = min(found[a, b], key=lambda t: (load[t[0]], max(t[1] % OWN, t[2] % OWN), t))
        load[m] += 1
        table[a, b] = m * 256 + i * 16 + j
        table[b, a] = m * 256 + j * 16 + i
    return table.reshape(-1)


HBM = pl.BlockSpec(memory_space=pl.ANY)
VM = pl.BlockSpec(memory_space=pltpu.VMEM)
SM = pl.BlockSpec(memory_space=pltpu.SMEM)
INFO = 2 + 2 * OVB


def params():
    return pltpu.CompilerParams(vmem_limit_bytes=56 * 1024 * 1024)


def halves(a):
    high = a.astype(BF16)
    return high, (a - high.astype(F32)).astype(BF16)


def dot(a, b, ca=1, cb=0):
    return lax.dot_general(a, b, (((ca,), (cb,)), ((), ())), preferred_element_type=F32)


def dot3(a, b, cb=0):
    (ah, al), (bh, bl) = a, b
    return dot(ah, bh, 1, cb) + (dot(ah, bl, 1, cb) + dot(al, bh, 1, cb))


def newton_schulz(ref, count):
    for i in range(count):
        m = ref[i]
        total = jnp.sum(jnp.sum(m * m, axis=1, keepdims=True), axis=0, keepdims=True)
        ref[i] = m * lax.rsqrt(total + 1e-6)

    def step(_, carry):
        ms = [ref[i] for i in range(count)]
        hs = [halves(m) for m in ms]
        squares = [dot3(h, h, 1) for h in hs]
        sh = [halves(s) for s in squares]
        polys = [coef_second * s + coef_third * dot3(h, h) for s, h in zip(squares, sh)]
        ph = [halves(p) for p in polys]
        for i in range(count):
            ref[i] = coef_first * ms[i] + dot3(ph[i], hs[i])
        return carry

    lax.fori_loop(0, NS_STEPS, step, 0)


def index_kernel(me_ref, table_ref, ends_ref, blocks_ref, info_ref, count_ref):
    me, base = me_ref[0], me_ref[1]

    def step(q, n):
        a, b = ends_ref[2 * q] - base, ends_ref[2 * q + 1] - base
        code = table_ref[(a >> 1) * DEVS + (b >> 1)]
        hit = (code >> 8) == me

        @pl.when(hit)
        def _():
            info_ref[n * INFO] = ((code >> 4) & 15) * PER + (a & 1)
            info_ref[n * INFO + 1] = (code & 15) * PER + (b & 1)
            for k in range(2 * OVB):
                info_ref[n * INFO + 2 + k] = blocks_ref[q * 2 * OVB + k]

        return n + jnp.where(hit, 1, 0)

    count_ref[0] = lax.fori_loop(0, ends_ref.shape[0] // 2, step, 0)


def make_index(me, table, ends, blocks):
    return pl.pallas_call(
        index_kernel,
        in_specs=[SM] * 4,
        out_specs=[SM] * 2,
        out_shape=[
            jax.ShapeDtypeStruct((MAX_PAIRS * INFO,), jnp.int32),
            jax.ShapeDtypeStruct((1,), jnp.int32),
        ],
        name="pair_index",
    )(me, table, ends, blocks)


def rotation_kernel(layout, info_ref, count_ref, *refs):
    arrays, (rot_ref, rows, mats, outs, load_sem, out_sem) = refs[:-6], refs[-6:]
    count = count_ref[0]
    batches = (count + BATCH - 1) // BATCH

    def block_ref(slot, block):
        number, part = layout[slot]
        ref = arrays[number]
        lines = pl.ds(pl.multiple_of(block * BLOCK, BLOCK), BLOCK)
        return ref.at[lines] if part is None else ref.at[part, lines]

    def load(batch, buf):
        def one(i, carry):
            j = jnp.minimum(batch * BATCH + i, count - 1)
            for e in range(2):
                slot = info_ref[j * INFO + e]
                for s in range(len(layout)):

                    @pl.when(slot == s)
                    def _():
                        for k in range(OVB):
                            pltpu.make_async_copy(
                                block_ref(s, info_ref[j * INFO + 2 + e * OVB + k]),
                                rows.at[buf, i, e, pl.ds(k * BLOCK, BLOCK)],
                                load_sem.at[buf],
                            ).start()

            return carry

        lax.fori_loop(0, BATCH, one, 0)

    def out_copy(batch):
        return pltpu.make_async_copy(outs, rot_ref.at[pl.ds(batch * BATCH, BATCH)], out_sem)

    @pl.when(batches > 0)
    def _():
        load(0, 0)

    def step(batch, carry):
        buf = batch & 1

        @pl.when(batch + 1 < batches)
        def _():
            load(batch + 1, 1 - buf)

        pltpu.make_async_copy(rows.at[buf], rows.at[buf], load_sem.at[buf]).wait()
        for i in range(BATCH):
            mats[i] = dot(rows[buf, i, 1], rows[buf, i, 0], 0, 0)
        newton_schulz(mats, BATCH)

        @pl.when(batch > 0)
        def _():
            out_copy(batch - 1).wait()

        for i in range(BATCH):
            outs[i] = mats[i]
        out_copy(batch).start()
        return carry

    lax.fori_loop(0, batches, step, 0)

    @pl.when(batches > 0)
    def _():
        out_copy(batches - 1).wait()


def make_rotations(info, count, arrays, layout):
    return pl.pallas_call(
        functools.partial(rotation_kernel, layout),
        in_specs=[SM, SM] + [HBM] * len(arrays),
        out_specs=HBM,
        out_shape=jax.ShapeDtypeStruct((MAX_PAIRS, D, D), F32),
        scratch_shapes=[
            pltpu.VMEM((2, BATCH, 2, OVB * BLOCK, D), BF16),
            pltpu.VMEM((BATCH, D, D), F32),
            pltpu.VMEM((BATCH, D, D), F32),
            pltpu.SemaphoreType.DMA((2,)),
            pltpu.SemaphoreType.DMA,
        ],
        compiler_params=params(),
        name="pair_rotations",
    )(info, count, *arrays)


def start_kernel(start_ref, frame_ref, low_ref):
    for p in range(PER):
        frame_ref[p] = start_ref[p]
    newton_schulz(frame_ref, PER)
    low_ref[...] = frame_ref[...].astype(BF16)


def make_start(start):
    return pl.pallas_call(
        start_kernel,
        in_specs=[VM],
        out_specs=[VM, VM],
        out_shape=[
            jax.ShapeDtypeStruct((PER, D, D), F32),
            jax.ShapeDtypeStruct((PER, D, D), BF16),
        ],
        compiler_params=params(),
        name="start_frames",
    )(start)


def estimate_kernel(info_ref, count_ref, rot_ref, *refs):
    lows = refs[:SLOTS]
    outs = refs[SLOTS : 2 * SLOTS]
    frames, acc, rot, frame_sem, rot_sem, out_sem = refs[2 * SLOTS :]
    count = count_ref[0]

    def rot_copy(j, buf):
        return pltpu.make_async_copy(rot_ref.at[j], rot.at[buf], rot_sem.at[buf])

    copies = [
        pltpu.make_async_copy(lows[s], frames.at[pl.ds(s * PER, PER)], frame_sem.at[s])
        for s in range(SLOTS)
    ]
    for copy in copies:
        copy.start()

    @pl.when(count > 0)
    def _():
        rot_copy(0, 0).start()

    acc[...] = jnp.zeros_like(acc)
    for copy in copies:
        copy.wait()

    def step(j, carry):
        buf = j & 1

        @pl.when(j + 1 < count)
        def _():
            rot_copy(j + 1, 1 - buf).start()

        rot_copy(j, buf).wait()
        sa, sb = info_ref[j * INFO], info_ref[j * INFO + 1]
        high, rest = halves(rot[buf])
        fa, fb = frames[sa], frames[sb]
        acc[sa] += dot(high, fb, 0, 0) + dot(rest, fb, 0, 0)
        acc[sb] += dot(high, fa) + dot(rest, fa)
        return carry

    lax.fori_loop(0, count, step, 0)
    copies = [
        pltpu.make_async_copy(acc.at[pl.ds(s * PER, PER)], outs[s], out_sem.at[s])
        for s in range(SLOTS)
    ]
    for copy in copies:
        copy.start()
    for copy in copies:
        copy.wait()


def make_estimates(info, count, rot, lows):
    return pl.pallas_call(
        estimate_kernel,
        in_specs=[SM, SM, HBM] + [HBM] * SLOTS,
        out_specs=[HBM] * SLOTS,
        out_shape=[jax.ShapeDtypeStruct((PER, D, D), F32)] * SLOTS,
        scratch_shapes=[
            pltpu.VMEM((SLOTS * PER, D, D), BF16),
            pltpu.VMEM((SLOTS * PER, D, D), F32),
            pltpu.VMEM((2, D, D), F32),
            pltpu.SemaphoreType.DMA((SLOTS,)),
            pltpu.SemaphoreType.DMA((2,)),
            pltpu.SemaphoreType.DMA((SLOTS,)),
        ],
        compiler_params=params(),
        name="estimates",
    )(info, count, rot, *lows)


def update_kernel(frame_ref, *refs):
    parts, (out_ref, low_ref, sum_ref) = refs[:-3], refs[-3:]
    for p in range(PER):
        total = frame_ref[p]
        for part in parts:
            total = total + part[p]
        out_ref[p] = total
    newton_schulz(out_ref, PER)
    low_ref[...] = out_ref[...].astype(BF16)
    sum_ref[...] = out_ref[0] + out_ref[1]


def make_update(frames, parts):
    return pl.pallas_call(
        update_kernel,
        in_specs=[VM] * (1 + len(parts)),
        out_specs=[VM] * 3,
        out_shape=[
            jax.ShapeDtypeStruct((PER, D, D), F32),
            jax.ShapeDtypeStruct((PER, D, D), BF16),
            jax.ShapeDtypeStruct((D, D), F32),
        ],
        compiler_params=params(),
        name="update_frames",
    )(frames, *parts)


CHUNK = 1024


def final_kernel(total_ref, frame_ref, patch_ref, aligned_ref, final_ref, gauge, rows, outs, low, in_sem, out_sem):
    chunks = [(p, pl.ds(r, CHUNK)) for p in range(PER) for r in range(0, patch_ref.shape[1], CHUNK)]
    ins = [
        pltpu.make_async_copy(patch_ref.at[p, r], rows.at[p, r], in_sem.at[n])
        for n, (p, r) in enumerate(chunks)
    ]
    for copy in ins:
        copy.start()
    gauge[0] = total_ref[...]
    newton_schulz(gauge, 1)
    g = halves(gauge[0])
    for p in range(PER):
        final = dot3(halves(frame_ref[p]), g, 1)
        final_ref[p] = final
        low[p] = final.astype(BF16)
    done = []
    for n, (p, r) in enumerate(chunks):
        ins[n].wait()
        outs[p, r] = dot(rows[p, r], low[p]).astype(BF16)
        copy = pltpu.make_async_copy(outs.at[p, r], aligned_ref.at[p, r], out_sem.at[n])
        copy.start()
        done.append(copy)
    for copy in done:
        copy.wait()


def make_final(total, frames, patches):
    pieces = PER * patches.shape[1] // CHUNK
    return pl.pallas_call(
        final_kernel,
        in_specs=[VM, VM, HBM],
        out_specs=[HBM, VM],
        out_shape=[
            jax.ShapeDtypeStruct(patches.shape, BF16),
            jax.ShapeDtypeStruct((PER, D, D), F32),
        ],
        scratch_shapes=[
            pltpu.VMEM((1, D, D), F32),
            pltpu.VMEM(patches.shape, BF16),
            pltpu.VMEM(patches.shape, BF16),
            pltpu.VMEM((PER, D, D), BF16),
            pltpu.SemaphoreType.DMA((pieces,)),
            pltpu.SemaphoreType.DMA((pieces,)),
        ],
        compiler_params=params(),
        name="aligned_rows",
    )(total, frames, patches)


def send(value, perm):
    return lax.ppermute(value, GY, perm)


def slot_perm(slot):
    src = sources()
    return [(src[m][slot], m) for m in range(DEVS)]


def spread_patches(patches):
    one = send(patches, step_perm(UP))
    four = send(patches, step_perm(LEFT))
    three_0 = send(patches[0], step_perm(RIGHT))
    two = send(one, step_perm(UP))
    five = send(four, step_perm(LEFT))
    cross_1 = send(one, SIBLING)
    cross_3_0 = send(three_0, SIBLING)
    three_1 = send(five[1], step_perm(LEFT))
    cross_2 = send(two, SIBLING)
    cross_3_1 = send(three_1, SIBLING)
    arrays = [patches, one, two, three_0, three_1, four, five, cross_1, cross_2, cross_3_0, cross_3_1]
    layout = (
        ((0, 0), (0, 1), (1, 0), (1, 1), (2, 0), (2, 1), (3, None), (4, None), (5, 0), (5, 1), (6, 0), (6, 1))
        + ((7, 0), (7, 1), (8, 0), (8, 1), (9, None), (10, None))
    )
    return arrays, layout


def spread_frames(low):
    return [low] + [send(low, slot_perm(s)) for s in range(1, SLOTS)]


def bring_back(parts):
    back = [parts[0]]
    for s in range(1, SLOTS):
        back.append(send(parts[s], [(m, d) for d, m in slot_perm(s)]))
    return back


def from_everyone(value, axis):
    size = lax.axis_size(axis)
    return lax.all_to_all(jnp.broadcast_to(value[None], (size, *value.shape)), axis, 0, 0, tiled=True)


def sum_over_all(value):
    size = lax.axis_size(GY)
    rows = value.shape[0] // size
    mine = lax.all_to_all(value.reshape(size, rows, D), GY, 0, 0, tiled=True).sum(0)
    mine = from_everyone(mine, "gx").sum(0)
    return from_everyone(mine, GY).reshape(value.shape)


def local(patches, start_frames, pair_ends, margin_blocks):
    me = lax.axis_index(GY).astype(jnp.int32)
    base = lax.axis_index("gx").astype(jnp.int32) * (DEVS * PER)
    arrays, layout = spread_patches(patches)
    info, count = make_index(
        jnp.stack([me, base]),
        jnp.asarray(meeting_table()),
        pair_ends.reshape(-1),
        margin_blocks.reshape(-1),
    )
    frames, low = make_start(start_frames)
    lows = spread_frames(low)
    rot = make_rotations(info, count, arrays, layout)
    for sweep in range(SWEEPS):
        if sweep:
            lows = spread_frames(low)
        back = bring_back(make_estimates(info, count, rot, lows))
        frames, low, frame_sum = make_update(frames, back)
    total = sum_over_all(frame_sum)
    aligned, final_frames = make_final(total, frames, patches)
    return aligned, final_frames, total


def solution(mesh):
    torus = Mesh(mesh.devices.reshape(mesh.shape["gx"], 4, 4, 2), ("gx", "gy_0", "gy_1", "gy_2"))
    return jax.shard_map(
        local,
        mesh=torus,
        in_specs=(P(GX_GY, None, None), P(GX_GY, None, None), P("gx", None), P("gx", None, None)),
        out_specs=(P(GX_GY, None, None), P(GX_GY, None, None), P()),
        check_vma=False,
    )
```

```python
import functools

import jax
import jax.numpy as jnp
import numpy as np
from jax import lax
from jax.experimental import pallas as pl
from jax.experimental.pallas import tpu as pltpu
from jax.sharding import Mesh
from jax.sharding import PartitionSpec as P


BLOCK = 128
OVB = 4
D = 256
SWEEPS = 2
NS_STEPS = 5
PER = 2
DEVS = 32
BATCH = 4
GY = ("gy_0", "gy_1", "gy_2")
GX_GY = ("gx", "gy_0", "gy_1", "gy_2")
F32, BF16 = jnp.float32, jnp.bfloat16

coef_first = 3.4445
coef_second = -4.775
coef_third = 2.0315

OFFS = (
    ((0, 0), (1, 0), (2, 0), (0, 1), (0, 3), (0, 2)),
    ((0, 0), (0, 1), (0, 2), (1, 0), (3, 0), (2, 0)),
)
CROSS = (1, 2, 3)
OWN = len(OFFS[0])
SLOTS = OWN + len(CROSS)
MAX_PAIRS = -(-(SLOTS * DEVS // 2) // BATCH) * BATCH


def device_at(z, x, c):
    return (z % 4) * 8 + (x % 4) * 2 + c % 2


def place_of(m):
    return m // 8, (m // 2) % 4, m % 2


def step_perm(steps):
    perm = []
    for m in range(DEVS):
        z, x, c = place_of(m)
        dz, dx = steps[c]
        perm.append((m, device_at(z + dz, x + dx, c)))
    return perm


def flip(step):
    return (step, (step[1], step[0]))


UP, RIGHT, LEFT = flip((1, 0)), flip((0, 1)), flip((0, -1))
SIBLING = [(m, m ^ 1) for m in range(DEVS)]


@functools.cache
def sources():
    same = []
    for m in range(DEVS):
        z, x, c = place_of(m)
        same.append([device_at(z - dz, x - dx, c) for dz, dx in OFFS[c]])
    return [same[m] + [same[m ^ 1][k] for k in CROSS] for m in range(DEVS)]


READY = ((0, 0), (0, 0), (1, 1), (0, 2), (0, 0), (1, 1), (0, 0), (1, 1), (0, 2))
CLASSES = 3
CHOICES = 3


@functools.cache
def meeting_table():
    found = {}
    src = sources()
    for m in range(DEVS):
        for i in range(SLOTS):
            for j in range(SLOTS):
                if src[m][i] != src[m][j]:
                    found.setdefault((src[m][i], src[m][j]), []).append((m, i, j))
    table = np.full((DEVS, PER, DEVS, PER, CHOICES), -1, np.int32)
    for (a, b), places in found.items():
        for pa in range(PER):
            for pb in range(PER):
                ranked = {}
                for m, i, j in places:
                    ready = max(READY[i][pa], READY[j][pb])
                    ranked[m] = min(ranked.get(m, (9,)), (ready, i, j))
                first = min(r[0] for r in ranked.values())
                codes = [
                    ((r * DEVS + m) << 8) | (i << 4) | j for m, (r, i, j) in sorted(ranked.items()) if r == first
                ]
                turn = (a + b) % len(codes)
                codes = (codes[turn:] + codes[:turn])[:CHOICES]
                codes += codes[-1:] * (CHOICES - len(codes))
                table[a, pa, b, pb] = codes
    return table.reshape(-1)


HBM = pl.BlockSpec(memory_space=pltpu.HBM)
VM = pl.BlockSpec(memory_space=pltpu.VMEM)
SM = pl.BlockSpec(memory_space=pltpu.SMEM)
INFO = 2 + 2 * OVB


def params():
    return pltpu.CompilerParams(vmem_limit_bytes=56 * 1024 * 1024)


def halves(a):
    high = a.astype(BF16)
    return high, (a - high.astype(F32)).astype(BF16)


def dot(a, b, ca=1, cb=0):
    return lax.dot_general(a, b, (((ca,), (cb,)), ((), ())), preferred_element_type=F32)


def dot3(a, b, cb=0):
    (ah, al), (bh, bl) = a, b
    return dot(ah, bh, 1, cb) + (dot(ah, bl, 1, cb) + dot(al, bh, 1, cb))


def newton_schulz(ref, count):
    for i in range(count):
        m = ref[i]
        total = jnp.sum(jnp.sum(m * m, axis=1, keepdims=True), axis=0, keepdims=True)
        ref[i] = m * lax.rsqrt(total + 1e-6)

    def step(_, carry):
        ms = [ref[i] for i in range(count)]
        hs = [halves(m) for m in ms]
        squares = [dot3(h, h, 1) for h in hs]
        sh = [halves(s) for s in squares]
        polys = [coef_second * s + coef_third * dot3(h, h) for s, h in zip(squares, sh)]
        ph = [halves(p) for p in polys]
        for i in range(count):
            ref[i] = coef_first * ms[i] + dot3(ph[i], hs[i])
        return carry

    lax.fori_loop(0, NS_STEPS, step, 0)


def index_kernel(me_ref, table_ref, ends_ref, blocks_ref, info_ref, count_ref, load_ref):
    me, base = me_ref[0], me_ref[1]
    for n in range(CLASSES * DEVS):
        load_ref[n] = 0

    def step(q, carry):
        a, b = ends_ref[2 * q] - base, ends_ref[2 * q + 1] - base
        first = (a * (DEVS * PER) + b) * CHOICES
        code = table_ref[first]
        least = load_ref[code >> 8]
        for k in range(1, CHOICES):
            other = table_ref[first + k]
            less = load_ref[other >> 8]
            code = jnp.where(less < least, other, code)
            least = jnp.minimum(less, least)
        place = code >> 8
        load_ref[place] = least + 1

        @pl.when((place & (DEVS - 1)) == me)
        def _():
            line = ((place >> 5) * MAX_PAIRS + least) * INFO
            info_ref[line] = ((code >> 4) & 15) * PER + (a & 1)
            info_ref[line + 1] = (code & 15) * PER + (b & 1)
            for k in range(2 * OVB):
                info_ref[line + 2 + k] = blocks_ref[q * 2 * OVB + k]

        return carry

    lax.fori_loop(0, ends_ref.shape[0] // 2, step, 0)
    for c in range(CLASSES):
        count_ref[c] = load_ref[c * DEVS + me]


def make_index(me, table, ends, blocks):
    return pl.pallas_call(
        index_kernel,
        in_specs=[SM] * 4,
        out_specs=[SM] * 2,
        out_shape=[
            jax.ShapeDtypeStruct((CLASSES * MAX_PAIRS * INFO,), jnp.int32),
            jax.ShapeDtypeStruct((CLASSES,), jnp.int32),
        ],
        scratch_shapes=[pltpu.SMEM((CLASSES * DEVS,), jnp.int32)],
        name="pair_index",
    )(me, table, ends, blocks)


def rotation_kernel(layout, ready, size, info_ref, count_ref, *refs):
    arrays, (rot_ref, rows, mats, outs, load_sem, out_sem) = refs[:-6], refs[-6:]
    count = count_ref[ready]
    first = jnp.int32(0)
    for c in range(ready):
        first = first + count_ref[c]
    batches = (count + size - 1) // size

    def block_ref(slot, block):
        number, part = layout[slot]
        ref = arrays[number]
        lines = pl.ds(pl.multiple_of(block * BLOCK, BLOCK), BLOCK)
        return ref.at[lines] if part is None else ref.at[part, lines]

    def load(batch, buf):
        def one(i, carry):
            line = (ready * MAX_PAIRS + jnp.minimum(batch * size + i, count - 1)) * INFO
            for e in range(2):
                slot = info_ref[line + e]
                for s in layout:

                    @pl.when(slot == s)
                    def _():
                        for k in range(OVB):
                            pltpu.make_async_copy(
                                block_ref(s, info_ref[line + 2 + e * OVB + k]),
                                rows.at[buf, i, e, pl.ds(k * BLOCK, BLOCK)],
                                load_sem.at[buf],
                            ).start()

            return carry

        lax.fori_loop(0, size, one, 0)

    def out_copy(batch):
        return pltpu.make_async_copy(outs, rot_ref.at[pl.ds(first + batch * size, size)], out_sem)

    @pl.when(batches > 0)
    def _():
        load(0, 0)

    def step(batch, carry):
        buf = batch & 1

        @pl.when(batch + 1 < batches)
        def _():
            load(batch + 1, 1 - buf)

        pltpu.make_async_copy(rows.at[buf], rows.at[buf], load_sem.at[buf]).wait()
        for i in range(size):
            mats[i] = dot(rows[buf, i, 1], rows[buf, i, 0], 0, 0)
        newton_schulz(mats, size)

        @pl.when(batch > 0)
        def _():
            out_copy(batch - 1).wait()

        for i in range(size):
            outs[i] = mats[i]
        out_copy(batch).start()
        return carry

    lax.fori_loop(0, batches, step, 0)

    @pl.when(batches > 0)
    def _():
        out_copy(batches - 1).wait()


def make_rotations(info, count, arrays, layout, ready, size, rot=None):
    layout = {s: at for s, at in enumerate(layout) if at[0] < len(arrays)}
    more = [] if rot is None else [rot]
    return pl.pallas_call(
        functools.partial(rotation_kernel, layout, ready, size),
        in_specs=[SM, SM] + [HBM] * (len(arrays) + len(more)),
        out_specs=HBM,
        out_shape=jax.ShapeDtypeStruct((MAX_PAIRS + BATCH, D, D), F32),
        input_output_aliases={2 + len(arrays): 0} if more else {},
        scratch_shapes=[
            pltpu.VMEM((2, size, 2, OVB * BLOCK, D), BF16),
            pltpu.VMEM((size, D, D), F32),
            pltpu.VMEM((size, D, D), F32),
            pltpu.SemaphoreType.DMA((2,)),
            pltpu.SemaphoreType.DMA,
        ],
        compiler_params=params(),
    )(info, count, *arrays, *more)


def start_kernel(start_ref, frame_ref, low_ref):
    for p in range(PER):
        frame_ref[p] = start_ref[p]
    newton_schulz(frame_ref, PER)
    low_ref[...] = frame_ref[...].astype(BF16)


def make_start(start):
    return pl.pallas_call(
        start_kernel,
        in_specs=[VM],
        out_specs=[VM, VM],
        out_shape=[
            jax.ShapeDtypeStruct((PER, D, D), F32),
            jax.ShapeDtypeStruct((PER, D, D), BF16),
        ],
        compiler_params=params(),
        name="start_frames",
    )(start)


def estimate_kernel(info_ref, count_ref, rot_ref, *refs):
    lows = refs[:SLOTS]
    outs = refs[SLOTS : SLOTS + OWN + 1]
    frames, acc, rot, frame_sem, rot_sem, out_sem = refs[SLOTS + OWN + 1 :]
    ends = [count_ref[0]]
    for c in range(1, CLASSES):
        ends.append(ends[-1] + count_ref[c])
    count = ends[-1]

    def line_of(j):
        line = j
        for c in range(1, CLASSES):
            line = jnp.where(j >= ends[c - 1], c * MAX_PAIRS + j - ends[c - 1], line)
        return line * INFO

    def rot_copy(j, buf):
        return pltpu.make_async_copy(rot_ref.at[j], rot.at[buf], rot_sem.at[buf])

    copies = [
        pltpu.make_async_copy(lows[s], frames.at[pl.ds(s * PER, PER)], frame_sem.at[s])
        for s in range(SLOTS)
    ]
    for copy in copies:
        copy.start()

    @pl.when(count > 0)
    def _():
        rot_copy(0, 0).start()

    acc[...] = jnp.zeros_like(acc)
    for copy in copies:
        copy.wait()

    def step(j, carry):
        buf = j & 1

        @pl.when(j + 1 < count)
        def _():
            rot_copy(j + 1, 1 - buf).start()

        rot_copy(j, buf).wait()
        line = line_of(j)
        sa, sb = info_ref[line], info_ref[line + 1]
        high, rest = halves(rot[buf])
        fa, fb = frames[sa], frames[sb]
        acc[sa] += dot(high, fb, 0, 0) + dot(rest, fb, 0, 0)
        acc[sb] += dot(high, fa) + dot(rest, fa)
        return carry

    lax.fori_loop(0, count, step, 0)
    parts = [(s * PER, PER) for s in range(OWN)] + [(OWN * PER, len(CROSS) * PER)]
    copies = [
        pltpu.make_async_copy(acc.at[pl.ds(*part)], outs[n], out_sem.at[n]) for n, part in enumerate(parts)
    ]
    for copy in copies:
        copy.start()
    for copy in copies:
        copy.wait()


def make_estimates(info, count, rot, lows):
    return pl.pallas_call(
        estimate_kernel,
        in_specs=[SM, SM, HBM] + [HBM] * SLOTS,
        out_specs=[HBM] * (OWN + 1),
        out_shape=[jax.ShapeDtypeStruct((PER, D, D), F32)] * OWN
        + [jax.ShapeDtypeStruct((len(CROSS) * PER, D, D), F32)],
        scratch_shapes=[
            pltpu.VMEM((SLOTS * PER, D, D), BF16),
            pltpu.VMEM((SLOTS * PER, D, D), F32),
            pltpu.VMEM((2, D, D), F32),
            pltpu.SemaphoreType.DMA((SLOTS,)),
            pltpu.SemaphoreType.DMA((2,)),
            pltpu.SemaphoreType.DMA((OWN + 1,)),
        ],
        compiler_params=params(),
        name="estimates",
    )(info, count, rot, *lows)


def update_kernel(frame_ref, *refs):
    parts, (out_ref, low_ref, sum_ref) = refs[:-3], refs[-3:]
    for p in range(PER):
        total = frame_ref[p]
        for part in parts:
            total = total + part[p]
        out_ref[p] = total
    newton_schulz(out_ref, PER)
    low_ref[...] = out_ref[...].astype(BF16)
    sum_ref[...] = out_ref[0] + out_ref[1]


def make_update(frames, parts):
    return pl.pallas_call(
        update_kernel,
        in_specs=[VM] * (1 + len(parts)),
        out_specs=[VM] * 3,
        out_shape=[
            jax.ShapeDtypeStruct((PER, D, D), F32),
            jax.ShapeDtypeStruct((PER, D, D), BF16),
            jax.ShapeDtypeStruct((D, D), F32),
        ],
        compiler_params=params(),
        name="update_frames",
    )(frames, *parts)


CHUNK = 1024


def final_kernel(total_ref, frame_ref, patch_ref, aligned_ref, final_ref, gauge, rows, outs, low, in_sem, out_sem):
    chunks = [(p, pl.ds(r, CHUNK)) for p in range(PER) for r in range(0, patch_ref.shape[1], CHUNK)]
    ins = [
        pltpu.make_async_copy(patch_ref.at[p, r], rows.at[p, r], in_sem.at[n])
        for n, (p, r) in enumerate(chunks)
    ]
    for copy in ins:
        copy.start()
    gauge[0] = total_ref[...]
    newton_schulz(gauge, 1)
    g = halves(gauge[0])
    for p in range(PER):
        final = dot3(halves(frame_ref[p]), g, 1)
        final_ref[p] = final
        low[p] = final.astype(BF16)
    done = []
    for n, (p, r) in enumerate(chunks):
        ins[n].wait()
        outs[p, r] = dot(rows[p, r], low[p]).astype(BF16)
        copy = pltpu.make_async_copy(outs.at[p, r], aligned_ref.at[p, r], out_sem.at[n])
        copy.start()
        done.append(copy)
    for copy in done:
        copy.wait()


def make_final(total, frames, patches):
    pieces = PER * patches.shape[1] // CHUNK
    return pl.pallas_call(
        final_kernel,
        in_specs=[VM, VM, HBM],
        out_specs=[HBM, VM],
        out_shape=[
            jax.ShapeDtypeStruct(patches.shape, BF16),
            jax.ShapeDtypeStruct((PER, D, D), F32),
        ],
        scratch_shapes=[
            pltpu.VMEM((1, D, D), F32),
            pltpu.VMEM(patches.shape, BF16),
            pltpu.VMEM(patches.shape, BF16),
            pltpu.VMEM((PER, D, D), BF16),
            pltpu.SemaphoreType.DMA((pieces,)),
            pltpu.SemaphoreType.DMA((pieces,)),
        ],
        compiler_params=params(),
        name="aligned_rows",
    )(total, frames, patches)


def send(value, perm):
    return lax.ppermute(value, GY, perm)


LAYOUT = (
    ((0, 0), (0, 1), (1, 0), (1, 1), (6, 0), (6, 1), (3, None), (9, None), (2, 0), (2, 1), (7, 0), (7, 1))
    + ((4, 0), (4, 1), (8, 0), (8, 1), (5, None), (10, None))
)


def back_perm(steps):
    return [(d, m) for m, d in step_perm(steps)]


def spread_frames(low):
    one, four, three = send(low, step_perm(UP)), send(low, step_perm(LEFT)), send(low, step_perm(RIGHT))
    two, five = send(one, step_perm(UP)), send(four, step_perm(LEFT))
    return [low, one, two, three, four, five] + [send(v, SIBLING) for v in (one, two, three)]


def bring_back(parts):
    own, one, two, three, four, five, cross = parts
    cross = send(cross, SIBLING)
    five = send(five, back_perm(LEFT))
    one, two, three = (v + cross[PER * n : PER * (n + 1)] for n, v in enumerate((one, two, three)))
    two = send(two, back_perm(UP))
    return [
        own,
        send(three, back_perm(RIGHT)),
        send(four + five, back_perm(LEFT)),
        send(one + two, back_perm(UP)),
    ]


def from_everyone(value, axis):
    size = lax.axis_size(axis)
    return lax.all_to_all(jnp.broadcast_to(value[None], (size, *value.shape)), axis, 0, 0, tiled=True)


def sum_over_all(value):
    size = lax.axis_size(GY)
    rows = value.shape[0] // size
    mine = lax.all_to_all(value.reshape(size, rows, D), GY, 0, 0, tiled=True).sum(0)
    mine = from_everyone(mine, "gx").sum(0)
    return from_everyone(mine, GY).reshape(value.shape)


def local(patches, start_frames, pair_ends, margin_blocks):
    me = lax.axis_index(GY).astype(jnp.int32)
    base = lax.axis_index("gx").astype(jnp.int32) * (DEVS * PER)
    one = send(patches, step_perm(UP))
    four = send(patches, step_perm(LEFT))
    three_0 = send(patches[0], step_perm(RIGHT))
    info, count = make_index(
        jnp.stack([me, base]),
        jnp.asarray(meeting_table()),
        pair_ends.reshape(-1),
        margin_blocks.reshape(-1),
    )
    frames, low = make_start(start_frames)
    lows = spread_frames(low)
    two = send(one, step_perm(UP))
    five = send(four, step_perm(LEFT))
    cross_1 = send(one, SIBLING)
    cross_3_0 = send(three_0, SIBLING)
    arrays = [patches, one, four, three_0, cross_1, cross_3_0]
    rot = make_rotations(info, count, arrays, LAYOUT, 0, BATCH)
    three_1 = send(five[1], step_perm(LEFT))
    cross_2 = send(two, SIBLING)
    arrays += [two, five, cross_2]
    rot = make_rotations(info, count, arrays, LAYOUT, 1, BATCH, rot)
    cross_3_1 = send(three_1, SIBLING)
    arrays += [three_1, cross_3_1]
    rot = make_rotations(info, count, arrays, LAYOUT, 2, 2, rot)
    for sweep in range(SWEEPS):
        if sweep:
            lows = spread_frames(low)
        back = bring_back(make_estimates(info, count, rot, lows))
        frames, low, frame_sum = make_update(frames, back)
    total = sum_over_all(frame_sum)
    aligned, final_frames = make_final(total, frames, patches)
    return aligned, final_frames, total


def solution(mesh):
    torus = Mesh(mesh.devices.reshape(mesh.shape["gx"], 4, 4, 2), ("gx", "gy_0", "gy_1", "gy_2"))
    return jax.shard_map(
        local,
        mesh=torus,
        in_specs=(P(GX_GY, None, None), P(GX_GY, None, None), P("gx", None), P("gx", None, None)),
        out_specs=(P(GX_GY, None, None), P(GX_GY, None, None), P()),
        check_vma=False,
    )
```

```python
import functools

import jax
import jax.numpy as jnp
import numpy as np
from jax import lax
from jax.experimental import pallas as pl
from jax.experimental.pallas import tpu as pltpu
from jax.sharding import Mesh
from jax.sharding import PartitionSpec as P


BLOCK = 128
OVB = 4
D = 256
SWEEPS = 2
NS_STEPS = 5
PER = 2
DEVS = 32
BATCH = 4
GY = ("gy_0", "gy_1", "gy_2")
GX_GY = ("gx", "gy_0", "gy_1", "gy_2")
F32, BF16 = jnp.float32, jnp.bfloat16

coef_first = 3.4445
coef_second = -4.775
coef_third = 2.0315

OFFS = (
    ((0, 0), (1, 0), (2, 0), (0, 1), (0, 3), (0, 2)),
    ((0, 0), (0, 1), (0, 2), (1, 0), (3, 0), (2, 0)),
)
CROSS = (1, 2, 3)
OWN = len(OFFS[0])
SLOTS = OWN + len(CROSS)
MAX_PAIRS = -(-(SLOTS * DEVS // 2) // BATCH) * BATCH


def device_at(z, x, c):
    return (z % 4) * 8 + (x % 4) * 2 + c % 2


def place_of(m):
    return m // 8, (m // 2) % 4, m % 2


def step_perm(steps):
    perm = []
    for m in range(DEVS):
        z, x, c = place_of(m)
        dz, dx = steps[c]
        perm.append((m, device_at(z + dz, x + dx, c)))
    return perm


def flip(step):
    return (step, (step[1], step[0]))


UP, RIGHT, LEFT = flip((1, 0)), flip((0, 1)), flip((0, -1))
SIBLING = [(m, m ^ 1) for m in range(DEVS)]


@functools.cache
def sources():
    same = []
    for m in range(DEVS):
        z, x, c = place_of(m)
        same.append([device_at(z - dz, x - dx, c) for dz, dx in OFFS[c]])
    return [same[m] + [same[m ^ 1][k] for k in CROSS] for m in range(DEVS)]


READY = ((0, 0), (0, 0), (1, 1), (2, 2), (0, 0), (1, 1), (0, 0), (1, 1), (2, 2))
CLASSES = 3
CHOICES = 3


@functools.cache
def meeting_table():
    found = {}
    src = sources()
    for m in range(DEVS):
        for i in range(SLOTS):
            for j in range(SLOTS):
                if src[m][i] != src[m][j]:
                    found.setdefault((src[m][i], src[m][j]), []).append((m, i, j))
    table = np.full((DEVS, PER, DEVS, PER, CHOICES), -1, np.int32)
    for (a, b), places in found.items():
        for pa in range(PER):
            for pb in range(PER):
                ranked = {}
                for m, i, j in places:
                    ready = max(READY[i][pa], READY[j][pb])
                    ranked[m] = min(ranked.get(m, (9,)), (ready, i, j))
                codes = [((r * DEVS + m) << 8) | (i << 4) | j for r, m, i, j in sorted((r, m, i, j) for m, (r, i, j) in ranked.items())]
                codes = codes[:CHOICES]
                codes += codes[-1:] * (CHOICES - len(codes))
                table[a, pa, b, pb] = codes
    return table.reshape(-1)


HBM = pl.BlockSpec(memory_space=pltpu.HBM)
VM = pl.BlockSpec(memory_space=pltpu.VMEM)
SM = pl.BlockSpec(memory_space=pltpu.SMEM)
INFO = 2 + 2 * OVB


def params():
    return pltpu.CompilerParams(vmem_limit_bytes=56 * 1024 * 1024)


def halves(a):
    high = a.astype(BF16)
    return high, (a - high.astype(F32)).astype(BF16)


def dot(a, b, ca=1, cb=0):
    return lax.dot_general(a, b, (((ca,), (cb,)), ((), ())), preferred_element_type=F32)


def dot3(a, b, cb=0):
    (ah, al), (bh, bl) = a, b
    return dot(ah, bh, 1, cb) + (dot(ah, bl, 1, cb) + dot(al, bh, 1, cb))


def newton_schulz(ref, count):
    for i in range(count):
        m = ref[i]
        total = jnp.sum(jnp.sum(m * m, axis=1, keepdims=True), axis=0, keepdims=True)
        ref[i] = m * lax.rsqrt(total + 1e-6)

    def step(_, carry):
        ms = [ref[i] for i in range(count)]
        hs = [halves(m) for m in ms]
        squares = [dot3(h, h, 1) for h in hs]
        sh = [halves(s) for s in squares]
        polys = [coef_second * s + coef_third * dot3(h, h) for s, h in zip(squares, sh)]
        ph = [halves(p) for p in polys]
        for i in range(count):
            ref[i] = coef_first * ms[i] + dot3(ph[i], hs[i])
        return carry

    lax.fori_loop(0, NS_STEPS, step, 0)


def index_kernel(me_ref, table_ref, ends_ref, blocks_ref, info_ref, count_ref, load_ref):
    me, base = me_ref[0], me_ref[1]
    for n in range((CLASSES + 1) * DEVS):
        load_ref[n] = 0

    def cost(code):
        place = code >> 8
        own = load_ref[place]
        late = jnp.where(place >= (CLASSES - 1) * DEVS, 2 * own + 4, 0)
        return own + late + load_ref[CLASSES * DEVS + (place & (DEVS - 1))]

    def step(q, carry):
        a, b = ends_ref[2 * q] - base, ends_ref[2 * q + 1] - base
        first = (a * (DEVS * PER) + b) * CHOICES
        code = table_ref[first]
        least = cost(code)
        for k in range(1, CHOICES):
            other = table_ref[first + k]
            less = cost(other)
            code = jnp.where(less < least, other, code)
            least = jnp.minimum(less, least)
        place = code >> 8
        device, ahead = place & (DEVS - 1), load_ref[place]
        load_ref[place] = ahead + 1
        load_ref[CLASSES * DEVS + device] += 1

        @pl.when(device == me)
        def _():
            line = ((place >> 5) * MAX_PAIRS + ahead) * INFO
            info_ref[line] = ((code >> 4) & 15) * PER + (a & 1)
            info_ref[line + 1] = (code & 15) * PER + (b & 1)
            for k in range(2 * OVB):
                info_ref[line + 2 + k] = blocks_ref[q * 2 * OVB + k]

        return carry

    lax.fori_loop(0, ends_ref.shape[0] // 2, step, 0)
    for c in range(CLASSES):
        count_ref[c] = load_ref[c * DEVS + me]


def make_index(me, table, ends, blocks):
    return pl.pallas_call(
        index_kernel,
        in_specs=[SM] * 4,
        out_specs=[SM] * 2,
        out_shape=[
            jax.ShapeDtypeStruct((CLASSES * MAX_PAIRS * INFO,), jnp.int32),
            jax.ShapeDtypeStruct((CLASSES,), jnp.int32),
        ],
        scratch_shapes=[pltpu.SMEM(((CLASSES + 1) * DEVS,), jnp.int32)],
        name="pair_index",
    )(me, table, ends, blocks)


def rotation_kernel(layout, ready, size, info_ref, count_ref, *refs):
    arrays, (rot_ref, rows, mats, outs, load_sem, out_sem) = refs[:-6], refs[-6:]
    count = count_ref[ready]
    first = jnp.int32(0)
    for c in range(ready):
        first = first + count_ref[c]
    batches = (count + size - 1) // size

    def block_ref(slot, block):
        number, part = layout[slot]
        ref = arrays[number]
        lines = pl.ds(pl.multiple_of(block * BLOCK, BLOCK), BLOCK)
        return ref.at[lines] if part is None else ref.at[part, lines]

    def load(batch, buf):
        def one(i, carry):
            line = (ready * MAX_PAIRS + jnp.minimum(batch * size + i, count - 1)) * INFO
            for e in range(2):
                slot = info_ref[line + e]
                for s in layout:

                    @pl.when(slot == s)
                    def _():
                        for k in range(OVB):
                            pltpu.make_async_copy(
                                block_ref(s, info_ref[line + 2 + e * OVB + k]),
                                rows.at[buf, i, e, pl.ds(k * BLOCK, BLOCK)],
                                load_sem.at[buf],
                            ).start()

            return carry

        lax.fori_loop(0, size, one, 0)

    def out_copy(batch):
        return pltpu.make_async_copy(outs, rot_ref.at[pl.ds(first + batch * size, size)], out_sem)

    @pl.when(batches > 0)
    def _():
        load(0, 0)

    def step(batch, carry):
        buf = batch & 1

        @pl.when(batch + 1 < batches)
        def _():
            load(batch + 1, 1 - buf)

        pltpu.make_async_copy(rows.at[buf], rows.at[buf], load_sem.at[buf]).wait()
        for i in range(size):
            mats[i] = dot(rows[buf, i, 1], rows[buf, i, 0], 0, 0)
        newton_schulz(mats, size)

        @pl.when(batch > 0)
        def _():
            out_copy(batch - 1).wait()

        for i in range(size):
            outs[i] = mats[i]
        out_copy(batch).start()
        return carry

    lax.fori_loop(0, batches, step, 0)

    @pl.when(batches > 0)
    def _():
        out_copy(batches - 1).wait()


def make_rotations(info, count, arrays, layout, ready, size, rot=None):
    layout = {s: at for s, at in enumerate(layout) if at[0] < len(arrays)}
    more = [] if rot is None else [rot]
    return pl.pallas_call(
        functools.partial(rotation_kernel, layout, ready, size),
        in_specs=[SM, SM] + [HBM] * (len(arrays) + len(more)),
        out_specs=HBM,
        out_shape=jax.ShapeDtypeStruct((MAX_PAIRS + BATCH, D, D), F32),
        input_output_aliases={2 + len(arrays): 0} if more else {},
        scratch_shapes=[
            pltpu.VMEM((2, size, 2, OVB * BLOCK, D), BF16),
            pltpu.VMEM((size, D, D), F32),
            pltpu.VMEM((size, D, D), F32),
            pltpu.SemaphoreType.DMA((2,)),
            pltpu.SemaphoreType.DMA,
        ],
        compiler_params=params(),
    )(info, count, *arrays, *more)


def start_kernel(start_ref, frame_ref, low_ref):
    for p in range(PER):
        frame_ref[p] = start_ref[p]
    newton_schulz(frame_ref, PER)
    low_ref[...] = frame_ref[...].astype(BF16)


def make_start(start):
    return pl.pallas_call(
        start_kernel,
        in_specs=[VM],
        out_specs=[VM, VM],
        out_shape=[
            jax.ShapeDtypeStruct((PER, D, D), F32),
            jax.ShapeDtypeStruct((PER, D, D), BF16),
        ],
        compiler_params=params(),
        name="start_frames",
    )(start)


def estimate_kernel(info_ref, count_ref, rot_ref, *refs):
    lows = refs[:SLOTS]
    outs = refs[SLOTS : SLOTS + OWN + 1]
    frames, acc, rot, frame_sem, rot_sem, out_sem = refs[SLOTS + OWN + 1 :]
    ends = [count_ref[0]]
    for c in range(1, CLASSES):
        ends.append(ends[-1] + count_ref[c])
    count = ends[-1]

    def line_of(j):
        line = j
        for c in range(1, CLASSES):
            line = jnp.where(j >= ends[c - 1], c * MAX_PAIRS + j - ends[c - 1], line)
        return line * INFO

    def rot_copy(t, buf):
        return pltpu.make_async_copy(rot_ref.at[pl.ds(2 * t, 2)], rot.at[buf], rot_sem.at[buf])

    copies = [
        pltpu.make_async_copy(lows[s], frames.at[pl.ds(s * PER, PER)], frame_sem.at[s])
        for s in range(SLOTS)
    ]
    for copy in copies:
        copy.start()

    @pl.when(count > 0)
    def _():
        rot_copy(0, 0).start()

    acc[...] = jnp.zeros_like(acc)
    for copy in copies:
        copy.wait()

    def step(t, carry):
        buf = t & 1

        @pl.when(2 * t + 2 < count)
        def _():
            rot_copy(t + 1, 1 - buf).start()

        rot_copy(t, buf).wait()
        found = []
        for i in range(2):
            line = line_of(jnp.minimum(2 * t + i, count - 1))
            sa, sb = info_ref[line], info_ref[line + 1]
            high, rest = halves(rot[buf, i])
            fa, fb = frames[sa], frames[sb]
            found.append((sa, dot(high, fb, 0, 0) + dot(rest, fb, 0, 0), sb, dot(high, fa) + dot(rest, fa)))

        def add(sa, ea, sb, eb):
            acc[sa] += ea
            acc[sb] += eb

        add(*found[0])

        @pl.when(2 * t + 1 < count)
        def _():
            add(*found[1])

        return carry

    lax.fori_loop(0, (count + 1) // 2, step, 0)
    parts = [(s * PER, PER) for s in range(OWN)] + [(OWN * PER, len(CROSS) * PER)]
    copies = [
        pltpu.make_async_copy(acc.at[pl.ds(*part)], outs[n], out_sem.at[n]) for n, part in enumerate(parts)
    ]
    for copy in copies:
        copy.start()
    for copy in copies:
        copy.wait()


def make_estimates(info, count, rot, lows):
    return pl.pallas_call(
        estimate_kernel,
        in_specs=[SM, SM, HBM] + [HBM] * SLOTS,
        out_specs=[HBM] * (OWN + 1),
        out_shape=[jax.ShapeDtypeStruct((PER, D, D), F32)] * OWN
        + [jax.ShapeDtypeStruct((len(CROSS) * PER, D, D), F32)],
        scratch_shapes=[
            pltpu.VMEM((SLOTS * PER, D, D), BF16),
            pltpu.VMEM((SLOTS * PER, D, D), F32),
            pltpu.VMEM((2, 2, D, D), F32),
            pltpu.SemaphoreType.DMA((SLOTS,)),
            pltpu.SemaphoreType.DMA((2,)),
            pltpu.SemaphoreType.DMA((OWN + 1,)),
        ],
        compiler_params=params(),
        name="estimates",
    )(info, count, rot, *lows)


def update_kernel(frame_ref, *refs):
    parts, (out_ref, low_ref, sum_ref) = refs[:-3], refs[-3:]
    for p in range(PER):
        total = frame_ref[p]
        for part in parts:
            total = total + part[p]
        out_ref[p] = total
    newton_schulz(out_ref, PER)
    low_ref[...] = out_ref[...].astype(BF16)
    sum_ref[...] = out_ref[0] + out_ref[1]


def make_update(frames, parts):
    return pl.pallas_call(
        update_kernel,
        in_specs=[VM] * (1 + len(parts)),
        out_specs=[VM] * 3,
        out_shape=[
            jax.ShapeDtypeStruct((PER, D, D), F32),
            jax.ShapeDtypeStruct((PER, D, D), BF16),
            jax.ShapeDtypeStruct((D, D), F32),
        ],
        compiler_params=params(),
        name="update_frames",
    )(frames, *parts)


CHUNK = 1024


def final_kernel(total_ref, frame_ref, patch_ref, aligned_ref, final_ref, gauge, rows, outs, low, in_sem, out_sem):
    chunks = [(p, pl.ds(r, CHUNK)) for p in range(PER) for r in range(0, patch_ref.shape[1], CHUNK)]
    ins = [
        pltpu.make_async_copy(patch_ref.at[p, r], rows.at[p, r], in_sem.at[n])
        for n, (p, r) in enumerate(chunks)
    ]
    for copy in ins:
        copy.start()
    gauge[0] = total_ref[...]
    newton_schulz(gauge, 1)
    g = halves(gauge[0])
    for p in range(PER):
        final = dot3(halves(frame_ref[p]), g, 1)
        final_ref[p] = final
        low[p] = final.astype(BF16)
    done = []
    for n, (p, r) in enumerate(chunks):
        ins[n].wait()
        outs[p, r] = dot(rows[p, r], low[p]).astype(BF16)
        copy = pltpu.make_async_copy(outs.at[p, r], aligned_ref.at[p, r], out_sem.at[n])
        copy.start()
        done.append(copy)
    for copy in done:
        copy.wait()


def make_final(total, frames, patches):
    pieces = PER * patches.shape[1] // CHUNK
    return pl.pallas_call(
        final_kernel,
        in_specs=[VM, VM, HBM],
        out_specs=[HBM, VM],
        out_shape=[
            jax.ShapeDtypeStruct(patches.shape, BF16),
            jax.ShapeDtypeStruct((PER, D, D), F32),
        ],
        scratch_shapes=[
            pltpu.VMEM((1, D, D), F32),
            pltpu.VMEM(patches.shape, BF16),
            pltpu.VMEM(patches.shape, BF16),
            pltpu.VMEM((PER, D, D), BF16),
            pltpu.SemaphoreType.DMA((pieces,)),
            pltpu.SemaphoreType.DMA((pieces,)),
        ],
        compiler_params=params(),
        name="aligned_rows",
    )(total, frames, patches)


def send(value, perm):
    return lax.ppermute(value, GY, perm)


LAYOUT = (
    ((0, 0), (0, 1), (1, 0), (1, 1), (4, 0), (4, 1), (7, None), (8, None), (2, 0), (2, 1), (5, 0), (5, 1))
    + ((3, 0), (3, 1), (6, 0), (6, 1), (9, None), (10, None))
)


def back_perm(steps):
    return [(d, m) for m, d in step_perm(steps)]


def spread_frames(low):
    one, four, three = send(low, step_perm(UP)), send(low, step_perm(LEFT)), send(low, step_perm(RIGHT))
    two, five = send(one, step_perm(UP)), send(four, step_perm(LEFT))
    return [low, one, two, three, four, five] + [send(v, SIBLING) for v in (one, two, three)]


def bring_back(parts):
    own, one, two, three, four, five, cross = parts
    cross = send(cross, SIBLING)
    five = send(five, back_perm(LEFT))
    one, two, three = (v + cross[PER * n : PER * (n + 1)] for n, v in enumerate((one, two, three)))
    two = send(two, back_perm(UP))
    return [
        own,
        send(three, back_perm(RIGHT)),
        send(four + five, back_perm(LEFT)),
        send(one + two, back_perm(UP)),
    ]


def from_everyone(value, axis):
    size = lax.axis_size(axis)
    return lax.all_to_all(jnp.broadcast_to(value[None], (size, *value.shape)), axis, 0, 0, tiled=True)


def sum_over_all(value):
    size = lax.axis_size(GY)
    rows = value.shape[0] // size
    mine = lax.all_to_all(value.reshape(size, rows, D), GY, 0, 0, tiled=True).sum(0)
    mine = from_everyone(mine, "gx").sum(0)
    return from_everyone(mine, GY).reshape(value.shape)


def local(patches, start_frames, pair_ends, margin_blocks):
    me = lax.axis_index(GY).astype(jnp.int32)
    base = lax.axis_index("gx").astype(jnp.int32) * (DEVS * PER)
    one = send(patches, step_perm(UP))
    four = send(patches, step_perm(LEFT))
    info, count = make_index(
        jnp.stack([me, base]),
        jnp.asarray(meeting_table()),
        pair_ends.reshape(-1),
        margin_blocks.reshape(-1),
    )
    frames, low = make_start(start_frames)
    lows = spread_frames(low)
    two = send(one, step_perm(UP))
    five = send(four, step_perm(LEFT))
    cross_1 = send(one, SIBLING)
    arrays = [patches, one, four, cross_1]
    rot = make_rotations(info, count, arrays, LAYOUT, 0, BATCH)
    three_0 = send(patches[0], step_perm(RIGHT))
    three_1 = send(five[1], step_perm(LEFT))
    cross_2 = send(two, SIBLING)
    arrays += [two, five, cross_2]
    rot = make_rotations(info, count, arrays, LAYOUT, 1, BATCH, rot)
    arrays += [three_0, three_1, send(three_0, SIBLING), send(three_1, SIBLING)]
    rot = make_rotations(info, count, arrays, LAYOUT, 2, 3, rot)
    for sweep in range(SWEEPS):
        if sweep:
            lows = spread_frames(low)
        back = bring_back(make_estimates(info, count, rot, lows))
        frames, low, frame_sum = make_update(frames, back)
    total = sum_over_all(frame_sum)
    aligned, final_frames = make_final(total, frames, patches)
    return aligned, final_frames, total


def solution(mesh):
    torus = Mesh(mesh.devices.reshape(mesh.shape["gx"], 4, 4, 2), ("gx", "gy_0", "gy_1", "gy_2"))
    return jax.shard_map(
        local,
        mesh=torus,
        in_specs=(P(GX_GY, None, None), P(GX_GY, None, None), P("gx", None), P("gx", None, None)),
        out_specs=(P(GX_GY, None, None), P(GX_GY, None, None), P()),
        check_vma=False,
    )
```

```python
import functools

import jax
import jax.numpy as jnp
import numpy as np
from jax import lax
from jax.experimental import pallas as pl
from jax.experimental.pallas import tpu as pltpu
from jax.sharding import Mesh
from jax.sharding import PartitionSpec as P


BLOCK = 128
OVB = 4
D = 256
SWEEPS = 2
NS_STEPS = 5
PER = 2
DEVS = 32
BATCH = 4
GY = ("gy_0", "gy_1", "gy_2")
GX_GY = ("gx", "gy_0", "gy_1", "gy_2")
F32, BF16 = jnp.float32, jnp.bfloat16

coef_first = 3.4445
coef_second = -4.775
coef_third = 2.0315

OFFS = (
    ((0, 0), (1, 0), (2, 0), (0, 1), (0, 3), (0, 2)),
    ((0, 0), (0, 1), (0, 2), (1, 0), (3, 0), (2, 0)),
)
CROSS = (1, 2, 3)
OWN = len(OFFS[0])
SLOTS = OWN + len(CROSS)
MAX_PAIRS = -(-(SLOTS * DEVS // 2) // BATCH) * BATCH


def device_at(z, x, c):
    return (z % 4) * 8 + (x % 4) * 2 + c % 2


def place_of(m):
    return m // 8, (m // 2) % 4, m % 2


def step_perm(steps):
    perm = []
    for m in range(DEVS):
        z, x, c = place_of(m)
        dz, dx = steps[c]
        perm.append((m, device_at(z + dz, x + dx, c)))
    return perm


def flip(step):
    return (step, (step[1], step[0]))


UP, RIGHT, LEFT = flip((1, 0)), flip((0, 1)), flip((0, -1))
SIBLING = [(m, m ^ 1) for m in range(DEVS)]


@functools.cache
def sources():
    same = []
    for m in range(DEVS):
        z, x, c = place_of(m)
        same.append([device_at(z - dz, x - dx, c) for dz, dx in OFFS[c]])
    return [same[m] + [same[m ^ 1][k] for k in CROSS] for m in range(DEVS)]


READY = ((0, 0), (0, 0), (1, 1), (2, 2), (0, 0), (1, 1), (0, 0), (1, 1), (2, 2))
CLASSES = 3
CHOICES = 3


@functools.cache
def meeting_table():
    found = {}
    src = sources()
    for m in range(DEVS):
        for i in range(SLOTS):
            for j in range(SLOTS):
                if src[m][i] != src[m][j]:
                    found.setdefault((src[m][i], src[m][j]), []).append((m, i, j))
    table = np.full((DEVS, PER, DEVS, PER, CHOICES), -1, np.int32)
    for (a, b), places in found.items():
        for pa in range(PER):
            for pb in range(PER):
                ranked = {}
                for m, i, j in places:
                    ready = max(READY[i][pa], READY[j][pb])
                    ranked[m] = min(ranked.get(m, (9,)), (ready, i, j))
                codes = [((r * DEVS + m) << 8) | (i << 4) | j for r, m, i, j in sorted((r, m, i, j) for m, (r, i, j) in ranked.items())]
                codes = codes[:CHOICES]
                codes += codes[-1:] * (CHOICES - len(codes))
                table[a, pa, b, pb] = codes
    return table.reshape(-1)


HBM = pl.BlockSpec(memory_space=pltpu.HBM)
VM = pl.BlockSpec(memory_space=pltpu.VMEM)
SM = pl.BlockSpec(memory_space=pltpu.SMEM)
INFO = 2 + 2 * OVB


def params(mib=56):
    return pltpu.CompilerParams(vmem_limit_bytes=mib * 1024 * 1024)


def halves(a):
    high = a.astype(BF16)
    return high, (a - high.astype(F32)).astype(BF16)


def dot(a, b, ca=1, cb=0):
    return lax.dot_general(a, b, (((ca,), (cb,)), ((), ())), preferred_element_type=F32)


def dot3(a, b, cb=0):
    (ah, al), (bh, bl) = a, b
    return dot(ah, bh, 1, cb) + (dot(ah, bl, 1, cb) + dot(al, bh, 1, cb))


def newton_schulz(ref, count):
    for i in range(count):
        m = ref[i]
        total = jnp.sum(jnp.sum(m * m, axis=1, keepdims=True), axis=0, keepdims=True)
        ref[i] = m * lax.rsqrt(total + 1e-6)

    def step(_, carry):
        ms = [ref[i] for i in range(count)]
        hs = [halves(m) for m in ms]
        squares = [dot3(h, h, 1) for h in hs]
        sh = [halves(s) for s in squares]
        polys = [coef_second * s + coef_third * dot3(h, h) for s, h in zip(squares, sh)]
        ph = [halves(p) for p in polys]
        for i in range(count):
            ref[i] = coef_first * ms[i] + dot3(ph[i], hs[i])
        return carry

    lax.fori_loop(0, NS_STEPS, step, 0)


def index_kernel(me_ref, table_ref, ends_ref, blocks_ref, info_ref, count_ref, load_ref):
    me, base = me_ref[0], me_ref[1]
    for n in range((CLASSES + 1) * DEVS):
        load_ref[n] = 0

    def cost(code):
        place = code >> 8
        own = load_ref[place]
        late = jnp.where(place >= (CLASSES - 1) * DEVS, 2 * own + 4, 0)
        return own + late + load_ref[CLASSES * DEVS + (place & (DEVS - 1))]

    def step(q, carry):
        a, b = ends_ref[2 * q] - base, ends_ref[2 * q + 1] - base
        first = (a * (DEVS * PER) + b) * CHOICES
        code = table_ref[first]
        least = cost(code)
        for k in range(1, CHOICES):
            other = table_ref[first + k]
            less = cost(other)
            code = jnp.where(less < least, other, code)
            least = jnp.minimum(less, least)
        place = code >> 8
        device, ahead = place & (DEVS - 1), load_ref[place]
        load_ref[place] = ahead + 1
        load_ref[CLASSES * DEVS + device] += 1

        @pl.when(device == me)
        def _():
            line = ((place >> 5) * MAX_PAIRS + ahead) * INFO
            info_ref[line] = ((code >> 4) & 15) * PER + (a & 1)
            info_ref[line + 1] = (code & 15) * PER + (b & 1)
            for k in range(2 * OVB):
                info_ref[line + 2 + k] = blocks_ref[q * 2 * OVB + k]

        return carry

    lax.fori_loop(0, ends_ref.shape[0] // 2, step, 0)
    for c in range(CLASSES):
        count_ref[c] = load_ref[c * DEVS + me]


def make_index(me, table, ends, blocks):
    return pl.pallas_call(
        index_kernel,
        in_specs=[SM] * 4,
        out_specs=[SM] * 2,
        out_shape=[
            jax.ShapeDtypeStruct((CLASSES * MAX_PAIRS * INFO,), jnp.int32),
            jax.ShapeDtypeStruct((CLASSES,), jnp.int32),
        ],
        scratch_shapes=[pltpu.SMEM(((CLASSES + 1) * DEVS,), jnp.int32)],
        name="pair_index",
    )(me, table, ends, blocks)


def rotation_kernel(layout, ready, size, info_ref, count_ref, *refs):
    arrays, (rot_ref, rows, mats, outs, load_sem, out_sem) = refs[:-6], refs[-6:]
    count = count_ref[ready]
    first = jnp.int32(0)
    for c in range(ready):
        first = first + count_ref[c]
    batches = (count + size - 1) // size

    def block_ref(slot, block):
        number, part = layout[slot]
        ref = arrays[number]
        lines = pl.ds(pl.multiple_of(block * BLOCK, BLOCK), BLOCK)
        return ref.at[lines] if part is None else ref.at[part, lines]

    def load(batch, buf):
        def one(i, carry):
            line = (ready * MAX_PAIRS + jnp.minimum(batch * size + i, count - 1)) * INFO
            for e in range(2):
                slot = info_ref[line + e]
                for s in layout:

                    @pl.when(slot == s)
                    def _():
                        for k in range(OVB):
                            pltpu.make_async_copy(
                                block_ref(s, info_ref[line + 2 + e * OVB + k]),
                                rows.at[buf, i, e, pl.ds(k * BLOCK, BLOCK)],
                                load_sem.at[buf],
                            ).start()

            return carry

        lax.fori_loop(0, size, one, 0)

    def out_copy(batch):
        return pltpu.make_async_copy(outs, rot_ref.at[pl.ds(first + batch * size, size)], out_sem)

    @pl.when(batches > 0)
    def _():
        load(0, 0)

    def step(batch, carry):
        buf = batch & 1

        @pl.when(batch + 1 < batches)
        def _():
            load(batch + 1, 1 - buf)

        pltpu.make_async_copy(rows.at[buf], rows.at[buf], load_sem.at[buf]).wait()
        for i in range(size):
            mats[i] = dot(rows[buf, i, 1], rows[buf, i, 0], 0, 0)
        newton_schulz(mats, size)

        @pl.when(batch > 0)
        def _():
            out_copy(batch - 1).wait()

        for i in range(size):
            outs[i] = mats[i]
        out_copy(batch).start()
        return carry

    lax.fori_loop(0, batches, step, 0)

    @pl.when(batches > 0)
    def _():
        out_copy(batches - 1).wait()


def make_rotations(info, count, arrays, layout, ready, size, rot=None):
    layout = {s: at for s, at in enumerate(layout) if at[0] < len(arrays)}
    more = [] if rot is None else [rot]
    return pl.pallas_call(
        functools.partial(rotation_kernel, layout, ready, size),
        in_specs=[SM, SM] + [HBM] * (len(arrays) + len(more)),
        out_specs=HBM,
        out_shape=jax.ShapeDtypeStruct((MAX_PAIRS + BATCH, D, D), F32),
        input_output_aliases={2 + len(arrays): 0} if more else {},
        scratch_shapes=[
            pltpu.VMEM((2, size, 2, OVB * BLOCK, D), BF16),
            pltpu.VMEM((size, D, D), F32),
            pltpu.VMEM((size, D, D), F32),
            pltpu.SemaphoreType.DMA((2,)),
            pltpu.SemaphoreType.DMA,
        ],
        compiler_params=params(60),
    )(info, count, *arrays, *more)


def start_kernel(start_ref, frame_ref, low_ref):
    for p in range(PER):
        frame_ref[p] = start_ref[p]
    newton_schulz(frame_ref, PER)
    low_ref[...] = frame_ref[...].astype(BF16)


def make_start(start):
    return pl.pallas_call(
        start_kernel,
        in_specs=[VM],
        out_specs=[VM, VM],
        out_shape=[
            jax.ShapeDtypeStruct((PER, D, D), F32),
            jax.ShapeDtypeStruct((PER, D, D), BF16),
        ],
        compiler_params=params(),
        name="start_frames",
    )(start)


def estimate_kernel(info_ref, count_ref, rot_ref, *refs):
    lows = refs[:SLOTS]
    outs = refs[SLOTS : SLOTS + OWN + 1]
    frames, acc, rot, frame_sem, rot_sem, out_sem = refs[SLOTS + OWN + 1 :]
    ends = [count_ref[0]]
    for c in range(1, CLASSES):
        ends.append(ends[-1] + count_ref[c])
    count = ends[-1]

    def line_of(j):
        line = j
        for c in range(1, CLASSES):
            line = jnp.where(j >= ends[c - 1], c * MAX_PAIRS + j - ends[c - 1], line)
        return line * INFO

    def rot_copy(t, buf):
        return pltpu.make_async_copy(rot_ref.at[pl.ds(2 * t, 2)], rot.at[buf], rot_sem.at[buf])

    copies = [
        pltpu.make_async_copy(lows[s], frames.at[pl.ds(s * PER, PER)], frame_sem.at[s])
        for s in range(SLOTS)
    ]
    for copy in copies:
        copy.start()

    @pl.when(count > 0)
    def _():
        rot_copy(0, 0).start()

    acc[...] = jnp.zeros_like(acc)
    for copy in copies:
        copy.wait()

    def step(t, carry):
        buf = t & 1

        @pl.when(2 * t + 2 < count)
        def _():
            rot_copy(t + 1, 1 - buf).start()

        rot_copy(t, buf).wait()
        found = []
        for i in range(2):
            line = line_of(jnp.minimum(2 * t + i, count - 1))
            sa, sb = info_ref[line], info_ref[line + 1]
            high, rest = halves(rot[buf, i])
            fa, fb = frames[sa], frames[sb]
            found.append((sa, dot(high, fb, 0, 0) + dot(rest, fb, 0, 0), sb, dot(high, fa) + dot(rest, fa)))

        def add(sa, ea, sb, eb):
            acc[sa] += ea
            acc[sb] += eb

        add(*found[0])

        @pl.when(2 * t + 1 < count)
        def _():
            add(*found[1])

        return carry

    lax.fori_loop(0, (count + 1) // 2, step, 0)
    parts = [(s * PER, PER) for s in range(OWN)] + [(OWN * PER, len(CROSS) * PER)]
    copies = [
        pltpu.make_async_copy(acc.at[pl.ds(*part)], outs[n], out_sem.at[n]) for n, part in enumerate(parts)
    ]
    for copy in copies:
        copy.start()
    for copy in copies:
        copy.wait()


def make_estimates(info, count, rot, lows):
    return pl.pallas_call(
        estimate_kernel,
        in_specs=[SM, SM, HBM] + [HBM] * SLOTS,
        out_specs=[HBM] * (OWN + 1),
        out_shape=[jax.ShapeDtypeStruct((PER, D, D), F32)] * OWN
        + [jax.ShapeDtypeStruct((len(CROSS) * PER, D, D), F32)],
        scratch_shapes=[
            pltpu.VMEM((SLOTS * PER, D, D), BF16),
            pltpu.VMEM((SLOTS * PER, D, D), F32),
            pltpu.VMEM((2, 2, D, D), F32),
            pltpu.SemaphoreType.DMA((SLOTS,)),
            pltpu.SemaphoreType.DMA((2,)),
            pltpu.SemaphoreType.DMA((OWN + 1,)),
        ],
        compiler_params=params(),
        name="estimates",
    )(info, count, rot, *lows)


def update_kernel(frame_ref, *refs):
    parts, (out_ref, low_ref, sum_ref) = refs[:-3], refs[-3:]
    for p in range(PER):
        total = frame_ref[p]
        for part in parts:
            total = total + part[p]
        out_ref[p] = total
    newton_schulz(out_ref, PER)
    low_ref[...] = out_ref[...].astype(BF16)
    sum_ref[...] = out_ref[0] + out_ref[1]


def make_update(frames, parts):
    return pl.pallas_call(
        update_kernel,
        in_specs=[VM] * (1 + len(parts)),
        out_specs=[VM] * 3,
        out_shape=[
            jax.ShapeDtypeStruct((PER, D, D), F32),
            jax.ShapeDtypeStruct((PER, D, D), BF16),
            jax.ShapeDtypeStruct((D, D), F32),
        ],
        compiler_params=params(),
        name="update_frames",
    )(frames, *parts)


CHUNK = 1024


def final_kernel(total_ref, frame_ref, patch_ref, aligned_ref, final_ref, gauge, rows, outs, low, in_sem, out_sem):
    pieces = patch_ref.shape[1] // CHUNK

    def piece(n):
        return n // pieces, pl.ds(pl.multiple_of(n % pieces * CHUNK, CHUNK), CHUNK)

    def copy_in(n):
        p, r = piece(n)
        return pltpu.make_async_copy(patch_ref.at[p, r], rows.at[p, r], in_sem.at[n])

    def copy_out(n):
        p, r = piece(n)
        return pltpu.make_async_copy(outs.at[p, r], aligned_ref.at[p, r], out_sem.at[n])

    for n in range(PER * pieces):
        copy_in(n).start()
    gauge[0] = total_ref[...]
    newton_schulz(gauge, 1)
    g = halves(gauge[0])
    for p in range(PER):
        final = dot3(halves(frame_ref[p]), g, 1)
        final_ref[p] = final
        low[p] = final.astype(BF16)

    def step(n, carry):
        p, r = piece(n)
        copy_in(n).wait()
        outs[p, r] = dot(rows[p, r], low[p]).astype(BF16)
        copy_out(n).start()
        return carry

    lax.fori_loop(0, PER * pieces, step, 0)
    for n in range(PER * pieces):
        copy_out(n).wait()


def make_final(total, frames, patches):
    pieces = PER * patches.shape[1] // CHUNK
    return pl.pallas_call(
        final_kernel,
        in_specs=[VM, VM, HBM],
        out_specs=[HBM, VM],
        out_shape=[
            jax.ShapeDtypeStruct(patches.shape, BF16),
            jax.ShapeDtypeStruct((PER, D, D), F32),
        ],
        scratch_shapes=[
            pltpu.VMEM((1, D, D), F32),
            pltpu.VMEM(patches.shape, BF16),
            pltpu.VMEM(patches.shape, BF16),
            pltpu.VMEM((PER, D, D), BF16),
            pltpu.SemaphoreType.DMA((pieces,)),
            pltpu.SemaphoreType.DMA((pieces,)),
        ],
        compiler_params=params(),
        name="aligned_rows",
    )(total, frames, patches)


def send(value, perm):
    return lax.ppermute(value, GY, perm)


LAYOUT = ((0, 0), (0, 1)) + tuple(
    (n + p, None) for n in (1, 7, 13, 3, 9, 5, 11, 15) for p in range(PER)
)


def back_perm(steps):
    return [(d, m) for m, d in step_perm(steps)]


def spread_frames(low):
    one, four, three = send(low, step_perm(UP)), send(low, step_perm(LEFT)), send(low, step_perm(RIGHT))
    two, five = send(one, step_perm(UP)), send(four, step_perm(LEFT))
    return [low, one, two, three, four, five] + [send(v, SIBLING) for v in (one, two, three)]


def bring_back(parts):
    own, one, two, three, four, five, cross = parts
    cross = send(cross, SIBLING)
    five = send(five, back_perm(LEFT))
    one, two, three = (v + cross[PER * n : PER * (n + 1)] for n, v in enumerate((one, two, three)))
    two = send(two, back_perm(UP))
    three = send(three, back_perm(RIGHT))
    return [own, three, send(four + five, back_perm(LEFT)), send(one + two, back_perm(UP))]


def axis_sum(value, axis):
    size = lax.axis_size(axis)

    def from_behind(hops):
        return lax.ppermute(value, axis, [(i, (i + hops) % size) for i in range(size)])

    near = from_behind(1), from_behind(-1)
    return (value + near[0]) + (near[1] + from_behind(2))


def sum_over_all(value):
    core = lax.axis_index("gy_2")
    swap = [(0, 1), (1, 0)]
    half = value.shape[0] // 2
    low, high = value[:half], value[half:]
    mine = jnp.where(core == 0, low, high) + lax.ppermute(jnp.where(core == 0, high, low), "gy_2", swap)
    for axis in ("gx", "gy_0", "gy_1"):
        mine = axis_sum(mine, axis)
    other = lax.ppermute(mine, "gy_2", swap)
    return jnp.concatenate([jnp.where(core == 0, mine, other), jnp.where(core == 0, other, mine)])


def local(patches, start_frames, pair_ends, margin_blocks):
    me = lax.axis_index(GY).astype(jnp.int32)
    base = lax.axis_index("gx").astype(jnp.int32) * (DEVS * PER)

    def hop(values, steps):
        out = [None] * PER
        for p in reversed(range(PER)):
            out[p] = send(values[p], step_perm(steps) if steps else SIBLING)
        return out

    both = [patches[p] for p in range(PER)]
    four = hop(both, LEFT)
    one = hop(both, UP)
    info, count = make_index(
        jnp.stack([me, base]),
        jnp.asarray(meeting_table()),
        pair_ends.reshape(-1),
        margin_blocks.reshape(-1),
    )
    frames, low = make_start(start_frames)
    lows = spread_frames(low)
    five = hop(four, LEFT)
    two = hop(one, UP)
    arrays = [patches, *one, *four, *hop(one, None)]
    rot = make_rotations(info, count, arrays, LAYOUT, 0, BATCH)
    three_0 = send(both[0], step_perm(RIGHT))
    three_1 = send(five[1], step_perm(LEFT))
    three = [three_0, three_1]
    arrays += [*two, *five, *hop(two, None)]
    rot = make_rotations(info, count, arrays, LAYOUT, 1, BATCH, rot)
    arrays += [*three, *hop(three, None)]
    rot = make_rotations(info, count, arrays, LAYOUT, 2, 3, rot)
    for sweep in range(SWEEPS):
        if sweep:
            lows = spread_frames(low)
        back = bring_back(make_estimates(info, count, rot, lows))
        frames, low, frame_sum = make_update(frames, back)
    total = sum_over_all(frame_sum)
    aligned, final_frames = make_final(total, frames, patches)
    return aligned, final_frames, total


def solution(mesh):
    torus = Mesh(mesh.devices.reshape(mesh.shape["gx"], 4, 4, 2), ("gx", "gy_0", "gy_1", "gy_2"))
    return jax.shard_map(
        local,
        mesh=torus,
        in_specs=(P(GX_GY, None, None), P(GX_GY, None, None), P("gx", None), P("gx", None, None)),
        out_specs=(P(GX_GY, None, None), P(GX_GY, None, None), P()),
        check_vma=False,
    )
```

```python
import functools

import jax
import jax.numpy as jnp
import numpy as np
from jax import lax
from jax.experimental import pallas as pl
from jax.experimental.pallas import tpu as pltpu
from jax.sharding import Mesh
from jax.sharding import PartitionSpec as P


BLOCK = 128
OVB = 4
D = 256
SWEEPS = 2
NS_STEPS = 5
PER = 2
DEVS = 32
BATCH = 4
GY = ("gy_0", "gy_1", "gy_2")
GX_GY = ("gx", "gy_0", "gy_1", "gy_2")
F32, BF16 = jnp.float32, jnp.bfloat16

coef_first = 3.4445
coef_second = -4.775
coef_third = 2.0315

OFFS = (
    ((0, 0), (1, 0), (2, 0), (0, 1), (0, 3), (0, 2)),
    ((0, 0), (0, 1), (0, 2), (1, 0), (3, 0), (2, 0)),
)
CROSS = (1, 2, 3)
OWN = len(OFFS[0])
SLOTS = OWN + len(CROSS)
MAX_PAIRS = -(-(SLOTS * DEVS // 2) // BATCH) * BATCH


def device_at(z, x, c):
    return (z % 4) * 8 + (x % 4) * 2 + c % 2


def place_of(m):
    return m // 8, (m // 2) % 4, m % 2


def step_perm(steps):
    perm = []
    for m in range(DEVS):
        z, x, c = place_of(m)
        dz, dx = steps[c]
        perm.append((m, device_at(z + dz, x + dx, c)))
    return perm


def flip(step):
    return (step, (step[1], step[0]))


UP, RIGHT, LEFT = flip((1, 0)), flip((0, 1)), flip((0, -1))
SIBLING = [(m, m ^ 1) for m in range(DEVS)]


@functools.cache
def sources():
    same = []
    for m in range(DEVS):
        z, x, c = place_of(m)
        same.append([device_at(z - dz, x - dx, c) for dz, dx in OFFS[c]])
    return [same[m] + [same[m ^ 1][k] for k in CROSS] for m in range(DEVS)]


READY = ((0, 0), (0, 0), (2, 1), (1, 2), (0, 0), (1, 1), (0, 0), (2, 1), (1, 2))
CLASSES = 3
CHOICES = 3


@functools.cache
def meeting_table():
    found = {}
    src = sources()
    for m in range(DEVS):
        for i in range(SLOTS):
            for j in range(SLOTS):
                if src[m][i] != src[m][j]:
                    found.setdefault((src[m][i], src[m][j]), []).append((m, i, j))
    table = np.full((DEVS, PER, DEVS, PER, CHOICES), -1, np.int32)
    for (a, b), places in found.items():
        for pa in range(PER):
            for pb in range(PER):
                ranked = {}
                for m, i, j in places:
                    ready = max(READY[i][pa], READY[j][pb])
                    ranked[m] = min(ranked.get(m, (9,)), (ready, i, j))
                codes = [((r * DEVS + m) << 8) | (i << 4) | j for r, m, i, j in sorted((r, m, i, j) for m, (r, i, j) in ranked.items())]
                codes = codes[:CHOICES]
                codes += codes[-1:] * (CHOICES - len(codes))
                table[a, pa, b, pb] = codes
    return table.reshape(-1)


HBM = pl.BlockSpec(memory_space=pltpu.HBM)
VM = pl.BlockSpec(memory_space=pltpu.VMEM)
SM = pl.BlockSpec(memory_space=pltpu.SMEM)
INFO = 2 + 2 * OVB


def params(mib=56):
    return pltpu.CompilerParams(vmem_limit_bytes=mib * 1024 * 1024)


def halves(a):
    high = a.astype(BF16)
    return high, (a - high.astype(F32)).astype(BF16)


def dot(a, b, ca=1, cb=0):
    return lax.dot_general(a, b, (((ca,), (cb,)), ((), ())), preferred_element_type=F32)


def dot3(a, b, cb=0):
    (ah, al), (bh, bl) = a, b
    return dot(ah, bh, 1, cb) + (dot(ah, bl, 1, cb) + dot(al, bh, 1, cb))


def newton_schulz(ref, count):
    for i in range(count):
        m = ref[i]
        total = jnp.sum(jnp.sum(m * m, axis=1, keepdims=True), axis=0, keepdims=True)
        ref[i] = m * lax.rsqrt(total + 1e-6)

    def step(_, carry):
        ms = [ref[i] for i in range(count)]
        hs = [halves(m) for m in ms]
        squares = [dot3(h, h, 1) for h in hs]
        sh = [halves(s) for s in squares]
        polys = [coef_second * s + coef_third * dot3(h, h) for s, h in zip(squares, sh)]
        ph = [halves(p) for p in polys]
        for i in range(count):
            ref[i] = coef_first * ms[i] + dot3(ph[i], hs[i])
        return carry

    lax.fori_loop(0, NS_STEPS, step, 0)


def index_kernel(me_ref, table_ref, ends_ref, blocks_ref, info_ref, count_ref, load_ref):
    me, base = me_ref[0], me_ref[1]
    for n in range((CLASSES + 1) * DEVS):
        load_ref[n] = 0

    def cost(code):
        place = code >> 8
        own = load_ref[place]
        late = jnp.where(place >= (CLASSES - 1) * DEVS, 2 * own + 4, 0)
        return own + late + load_ref[CLASSES * DEVS + (place & (DEVS - 1))]

    def step(q, carry):
        a, b = ends_ref[2 * q] - base, ends_ref[2 * q + 1] - base
        first = (a * (DEVS * PER) + b) * CHOICES
        code = table_ref[first]
        least = cost(code)
        for k in range(1, CHOICES):
            other = table_ref[first + k]
            less = cost(other)
            code = jnp.where(less < least, other, code)
            least = jnp.minimum(less, least)
        place = code >> 8
        device, ahead = place & (DEVS - 1), load_ref[place]
        load_ref[place] = ahead + 1
        load_ref[CLASSES * DEVS + device] += 1

        @pl.when(device == me)
        def _():
            line = ((place >> 5) * MAX_PAIRS + ahead) * INFO
            info_ref[line] = ((code >> 4) & 15) * PER + (a & 1)
            info_ref[line + 1] = (code & 15) * PER + (b & 1)
            for k in range(2 * OVB):
                info_ref[line + 2 + k] = blocks_ref[q * 2 * OVB + k]

        return carry

    lax.fori_loop(0, ends_ref.shape[0] // 2, step, 0)
    for c in range(CLASSES):
        count_ref[c] = load_ref[c * DEVS + me]


def make_index(me, table, ends, blocks):
    return pl.pallas_call(
        index_kernel,
        in_specs=[SM] * 4,
        out_specs=[SM] * 2,
        out_shape=[
            jax.ShapeDtypeStruct((CLASSES * MAX_PAIRS * INFO,), jnp.int32),
            jax.ShapeDtypeStruct((CLASSES,), jnp.int32),
        ],
        scratch_shapes=[pltpu.SMEM(((CLASSES + 1) * DEVS,), jnp.int32)],
        name="pair_index",
    )(me, table, ends, blocks)


def rotation_kernel(layout, ready, size, info_ref, count_ref, *refs):
    arrays, (rot_ref, rows, mats, outs, load_sem, out_sem) = refs[:-6], refs[-6:]
    count = count_ref[ready]
    first = jnp.int32(0)
    for c in range(ready):
        first = first + count_ref[c]
    batches = (count + size - 1) // size

    def block_ref(slot, block):
        number, part = layout[slot]
        ref = arrays[number]
        lines = pl.ds(pl.multiple_of(block * BLOCK, BLOCK), BLOCK)
        return ref.at[lines] if part is None else ref.at[part, lines]

    def load(batch, buf):
        def one(i, carry):
            line = (ready * MAX_PAIRS + jnp.minimum(batch * size + i, count - 1)) * INFO
            for e in range(2):
                slot = info_ref[line + e]
                for s in layout:

                    @pl.when(slot == s)
                    def _():
                        for k in range(OVB):
                            pltpu.make_async_copy(
                                block_ref(s, info_ref[line + 2 + e * OVB + k]),
                                rows.at[buf, i, e, pl.ds(k * BLOCK, BLOCK)],
                                load_sem.at[buf],
                            ).start()

            return carry

        lax.fori_loop(0, size, one, 0)

    def out_copy(batch):
        return pltpu.make_async_copy(outs, rot_ref.at[pl.ds(first + batch * size, size)], out_sem)

    @pl.when(batches > 0)
    def _():
        load(0, 0)

    def step(batch, carry):
        buf = batch & 1

        @pl.when(batch + 1 < batches)
        def _():
            load(batch + 1, 1 - buf)

        pltpu.make_async_copy(rows.at[buf], rows.at[buf], load_sem.at[buf]).wait()
        for i in range(size):
            mats[i] = dot(rows[buf, i, 1], rows[buf, i, 0], 0, 0)
        newton_schulz(mats, size)

        @pl.when(batch > 0)
        def _():
            out_copy(batch - 1).wait()

        for i in range(size):
            outs[i] = mats[i]
        out_copy(batch).start()
        return carry

    lax.fori_loop(0, batches, step, 0)

    @pl.when(batches > 0)
    def _():
        out_copy(batches - 1).wait()


def make_rotations(info, count, arrays, layout, ready, size, rot=None):
    layout = {s: at for s, at in enumerate(layout) if at[0] < len(arrays)}
    more = [] if rot is None else [rot]
    return pl.pallas_call(
        functools.partial(rotation_kernel, layout, ready, size),
        in_specs=[SM, SM] + [HBM] * (len(arrays) + len(more)),
        out_specs=HBM,
        out_shape=jax.ShapeDtypeStruct((MAX_PAIRS + BATCH, D, D), F32),
        input_output_aliases={2 + len(arrays): 0} if more else {},
        scratch_shapes=[
            pltpu.VMEM((2, size, 2, OVB * BLOCK, D), BF16),
            pltpu.VMEM((size, D, D), F32),
            pltpu.VMEM((size, D, D), F32),
            pltpu.SemaphoreType.DMA((2,)),
            pltpu.SemaphoreType.DMA,
        ],
        compiler_params=params(60),
    )(info, count, *arrays, *more)


def start_kernel(start_ref, frame_ref, low_ref):
    for p in range(PER):
        frame_ref[p] = start_ref[p]
    newton_schulz(frame_ref, PER)
    low_ref[...] = frame_ref[...].astype(BF16)


def make_start(start):
    return pl.pallas_call(
        start_kernel,
        in_specs=[VM],
        out_specs=[VM, VM],
        out_shape=[
            jax.ShapeDtypeStruct((PER, D, D), F32),
            jax.ShapeDtypeStruct((PER, D, D), BF16),
        ],
        compiler_params=params(),
        name="start_frames",
    )(start)


def estimate_kernel(info_ref, count_ref, rot_ref, *refs):
    lows = refs[:SLOTS]
    outs = refs[SLOTS : SLOTS + OWN + 1]
    frames, acc, rot, frame_sem, rot_sem, out_sem = refs[SLOTS + OWN + 1 :]
    ends = [count_ref[0]]
    for c in range(1, CLASSES):
        ends.append(ends[-1] + count_ref[c])
    count = ends[-1]

    def line_of(j):
        line = j
        for c in range(1, CLASSES):
            line = jnp.where(j >= ends[c - 1], c * MAX_PAIRS + j - ends[c - 1], line)
        return line * INFO

    def rot_copy(t, buf):
        return pltpu.make_async_copy(rot_ref.at[pl.ds(2 * t, 2)], rot.at[buf], rot_sem.at[buf])

    copies = [
        pltpu.make_async_copy(lows[s], frames.at[pl.ds(s * PER, PER)], frame_sem.at[s])
        for s in range(SLOTS)
    ]
    for copy in copies:
        copy.start()

    @pl.when(count > 0)
    def _():
        rot_copy(0, 0).start()

    acc[...] = jnp.zeros_like(acc)
    for copy in copies:
        copy.wait()

    def step(t, carry):
        buf = t & 1

        @pl.when(2 * t + 2 < count)
        def _():
            rot_copy(t + 1, 1 - buf).start()

        rot_copy(t, buf).wait()
        found = []
        for i in range(2):
            line = line_of(jnp.minimum(2 * t + i, count - 1))
            sa, sb = info_ref[line], info_ref[line + 1]
            high, rest = halves(rot[buf, i])
            fa, fb = frames[sa], frames[sb]
            found.append((sa, dot(high, fb, 0, 0) + dot(rest, fb, 0, 0), sb, dot(high, fa) + dot(rest, fa)))

        def add(sa, ea, sb, eb):
            acc[sa] += ea
            acc[sb] += eb

        add(*found[0])

        @pl.when(2 * t + 1 < count)
        def _():
            add(*found[1])

        return carry

    lax.fori_loop(0, (count + 1) // 2, step, 0)
    parts = [(s * PER, PER) for s in range(OWN)] + [(OWN * PER, len(CROSS) * PER)]
    copies = [
        pltpu.make_async_copy(acc.at[pl.ds(*part)], outs[n], out_sem.at[n]) for n, part in enumerate(parts)
    ]
    for copy in copies:
        copy.start()
    for copy in copies:
        copy.wait()


def make_estimates(info, count, rot, lows):
    return pl.pallas_call(
        estimate_kernel,
        in_specs=[SM, SM, HBM] + [HBM] * SLOTS,
        out_specs=[HBM] * (OWN + 1),
        out_shape=[jax.ShapeDtypeStruct((PER, D, D), F32)] * OWN
        + [jax.ShapeDtypeStruct((len(CROSS) * PER, D, D), F32)],
        scratch_shapes=[
            pltpu.VMEM((SLOTS * PER, D, D), BF16),
            pltpu.VMEM((SLOTS * PER, D, D), F32),
            pltpu.VMEM((2, 2, D, D), F32),
            pltpu.SemaphoreType.DMA((SLOTS,)),
            pltpu.SemaphoreType.DMA((2,)),
            pltpu.SemaphoreType.DMA((OWN + 1,)),
        ],
        compiler_params=params(),
        name="estimates",
    )(info, count, rot, *lows)


def update_kernel(core_ref, frame_ref, *refs):
    parts, (out_ref, *more) = refs[: OWN - 2], refs[OWN - 2 :]
    for p in range(PER):
        total = frame_ref[p]
        for part in parts:
            total = total + part[p]
        out_ref[p] = total
    newton_schulz(out_ref, PER)
    if len(more) == 1:
        more[0][...] = out_ref[...].astype(BF16)
    else:
        for ref, half in zip(more, (core_ref[0], 1 - core_ref[0])):
            rows = pl.ds(pl.multiple_of(half * (D // 2), D // 2), D // 2)
            ref[...] = out_ref[0, rows] + out_ref[1, rows]


def make_update(frames, parts, core=None):
    more = [jax.ShapeDtypeStruct((PER, D, D), BF16)]
    if core is not None:
        more = [jax.ShapeDtypeStruct((D // 2, D), F32)] * 2
    return pl.pallas_call(
        update_kernel,
        in_specs=[SM] + [VM] * (1 + len(parts)),
        out_specs=[VM] * (1 + len(more)),
        out_shape=[jax.ShapeDtypeStruct((PER, D, D), F32)] + more,
        compiler_params=params(),
        name="update_frames",
    )(jnp.zeros(1, jnp.int32) if core is None else core, frames, *parts)


CHUNK = 1024


def final_kernel(
    core_ref, keep_ref, other_ref, frame_ref, patch_ref, aligned_ref, final_ref, total_ref, gauge, rows, outs, low, in_sem, out_sem
):
    pieces = patch_ref.shape[1] // CHUNK

    def piece(n):
        return n // pieces, pl.ds(pl.multiple_of(n % pieces * CHUNK, CHUNK), CHUNK)

    def copy_in(n):
        p, r = piece(n)
        return pltpu.make_async_copy(patch_ref.at[p, r], rows.at[p, r], in_sem.at[n])

    def copy_out(n):
        p, r = piece(n)
        return pltpu.make_async_copy(outs.at[p, r], aligned_ref.at[p, r], out_sem.at[n])

    for n in range(PER * pieces):
        copy_in(n).start()
    for ref, half in ((keep_ref, core_ref[0]), (other_ref, 1 - core_ref[0])):
        total_ref[pl.ds(pl.multiple_of(half * (D // 2), D // 2), D // 2)] = ref[...]
    gauge[0] = total_ref[...]
    newton_schulz(gauge, 1)
    g = halves(gauge[0])
    for p in range(PER):
        final = dot3(halves(frame_ref[p]), g, 1)
        final_ref[p] = final
        low[p] = final.astype(BF16)

    def step(n, carry):
        p, r = piece(n)
        copy_in(n).wait()
        outs[p, r] = dot(rows[p, r], low[p]).astype(BF16)
        copy_out(n).start()
        return carry

    lax.fori_loop(0, PER * pieces, step, 0)
    for n in range(PER * pieces):
        copy_out(n).wait()


def make_final(core, keep, other, frames, patches):
    pieces = PER * patches.shape[1] // CHUNK
    return pl.pallas_call(
        final_kernel,
        in_specs=[SM, VM, VM, VM, HBM],
        out_specs=[HBM, VM, VM],
        out_shape=[
            jax.ShapeDtypeStruct(patches.shape, BF16),
            jax.ShapeDtypeStruct((PER, D, D), F32),
            jax.ShapeDtypeStruct((D, D), F32),
        ],
        scratch_shapes=[
            pltpu.VMEM((1, D, D), F32),
            pltpu.VMEM(patches.shape, BF16),
            pltpu.VMEM(patches.shape, BF16),
            pltpu.VMEM((PER, D, D), BF16),
            pltpu.SemaphoreType.DMA((pieces,)),
            pltpu.SemaphoreType.DMA((pieces,)),
        ],
        compiler_params=params(),
        name="aligned_rows",
    )(core, keep, other, frames, patches)


def send(value, perm):
    return lax.ppermute(value, GY, perm)


LAYOUT = ((0, 0), (0, 1)) + tuple(
    (n, None) for n in (1, 2, 13, 7, 10, 14, 3, 4, 8, 9, 5, 6, 15, 11, 12, 16)
)


def back_perm(steps):
    return [(d, m) for m, d in step_perm(steps)]


def spread_frames(low):
    one, four, three = send(low, step_perm(UP)), send(low, step_perm(LEFT)), send(low, step_perm(RIGHT))
    two, five = send(one, step_perm(UP)), send(four, step_perm(LEFT))
    return [low, one, two, three, four, five] + [send(v, SIBLING) for v in (one, two, three)]


def bring_back(parts):
    own, one, two, three, four, five, cross = parts
    cross = send(cross, SIBLING)
    five = send(five, back_perm(LEFT))
    one, two, three = (
        lax.optimization_barrier(v + cross[PER * n : PER * (n + 1)]) for n, v in enumerate((one, two, three))
    )
    two = send(two, back_perm(UP))
    three = send(three, back_perm(RIGHT))
    return [own, three, send(four + five, back_perm(LEFT)), send(one + two, back_perm(UP))]


def axis_sum(value, axis):
    size = lax.axis_size(axis)

    def from_behind(hops):
        return lax.ppermute(value, axis, [(i, (i + hops) % size) for i in range(size)])

    near = from_behind(1), from_behind(-1)
    return (value + near[0]) + (near[1] + from_behind(2))


def sum_over_all(keep, give):
    swap = [(0, 1), (1, 0)]
    keep = keep + lax.ppermute(give, "gy_2", swap)
    for axis in ("gx", "gy_0", "gy_1"):
        keep = axis_sum(keep, axis)
    return keep, lax.ppermute(keep, "gy_2", swap)


def local(patches, start_frames, pair_ends, margin_blocks):
    me = lax.axis_index(GY).astype(jnp.int32)
    base = lax.axis_index("gx").astype(jnp.int32) * (DEVS * PER)

    def move(value, steps=None):
        return send(value, step_perm(steps) if steps else SIBLING)

    upper = patches[1]
    four_1, one_1 = move(upper, LEFT), move(upper, UP)
    lower = lax.optimization_barrier(patches)[0]
    four_0, one_0 = move(lower, LEFT), move(lower, UP)
    info, count = make_index(
        jnp.stack([me, base]),
        jnp.asarray(meeting_table()),
        pair_ends.reshape(-1),
        margin_blocks.reshape(-1),
    )
    frames, low = make_start(start_frames)
    lows = spread_frames(low)
    five_1, two_1 = move(four_1, LEFT), move(one_1, UP)
    five_0, two_0 = move(four_0, LEFT), move(one_0, UP)
    three_0 = move(lower, RIGHT)
    arrays = [patches, one_0, one_1, four_0, four_1, move(one_0), move(one_1)]
    rot = make_rotations(info, count, arrays, LAYOUT, 0, BATCH)
    three_1 = move(five_1, LEFT)
    arrays += [two_1, five_0, five_1, three_0, move(two_1), move(three_0)]
    rot = make_rotations(info, count, arrays, LAYOUT, 1, BATCH, rot)
    arrays += [two_0, three_1, move(two_0), move(three_1)]
    rot = make_rotations(info, count, arrays, LAYOUT, 2, BATCH, rot)
    core = lax.axis_index("gy_2").astype(jnp.int32).reshape(1)
    for sweep in range(SWEEPS):
        if sweep:
            lows = spread_frames(low)
        back = bring_back(make_estimates(info, count, rot, lows))
        if sweep < SWEEPS - 1:
            frames, low = make_update(frames, back)
        else:
            frames, keep, give = make_update(frames, back, core)
    keep, other = sum_over_all(keep, give)
    aligned, final_frames, total = make_final(core, keep, other, frames, patches)
    return aligned, final_frames, total


def solution(mesh):
    torus = Mesh(mesh.devices.reshape(mesh.shape["gx"], 4, 4, 2), ("gx", "gy_0", "gy_1", "gy_2"))
    return jax.shard_map(
        local,
        mesh=torus,
        in_specs=(P(GX_GY, None, None), P(GX_GY, None, None), P("gx", None), P("gx", None, None)),
        out_specs=(P(GX_GY, None, None), P(GX_GY, None, None), P()),
        check_vma=False,
    )
```

```python
import functools

import jax
import jax.numpy as jnp
import numpy as np
from jax import lax
from jax.experimental import pallas as pl
from jax.experimental.pallas import tpu as pltpu
from jax.sharding import Mesh
from jax.sharding import PartitionSpec as P


BLOCK = 128
OVB = 4
D = 256
SWEEPS = 2
NS_STEPS = 5
PER = 2
DEVS = 32
GY = ("gy_0", "gy_1", "gy_2")
GX_GY = ("gx", "gy_0", "gy_1", "gy_2")
F32, BF16 = jnp.float32, jnp.bfloat16

coef_first = 3.4445
coef_second = -4.775
coef_third = 2.0315

OFFS = (
    ((0, 0), (1, 0), (2, 0), (0, 1), (0, 3), (0, 2)),
    ((0, 0), (0, 1), (0, 2), (1, 0), (3, 0), (2, 0)),
)
CROSS = (1, 2, 3)
OWN = len(OFFS[0])
SLOTS = OWN + len(CROSS)
MAX_PAIRS = SLOTS * DEVS // 2


def device_at(z, x, c):
    return (z % 4) * 8 + (x % 4) * 2 + c % 2


def place_of(m):
    return m // 8, (m // 2) % 4, m % 2


def step_perm(steps):
    perm = []
    for m in range(DEVS):
        z, x, c = place_of(m)
        dz, dx = steps[c]
        perm.append((m, device_at(z + dz, x + dx, c)))
    return perm


def flip(step):
    return (step, (step[1], step[0]))


UP, RIGHT, LEFT = flip((1, 0)), flip((0, 1)), flip((0, -1))
SIBLING = [(m, m ^ 1) for m in range(DEVS)]


@functools.cache
def sources():
    same = []
    for m in range(DEVS):
        z, x, c = place_of(m)
        same.append([device_at(z - dz, x - dx, c) for dz, dx in OFFS[c]])
    return [same[m] + [same[m ^ 1][k] for k in CROSS] for m in range(DEVS)]


READY = ((0, 0), (0, 0), (2, 1), (1, 2), (0, 0), (1, 1), (0, 0), (2, 1), (1, 2))
CLASSES = 3
CHOICES = 3


@functools.cache
def meeting_table():
    found = {}
    src = sources()
    for m in range(DEVS):
        for i in range(SLOTS):
            for j in range(SLOTS):
                if src[m][i] != src[m][j]:
                    found.setdefault((src[m][i], src[m][j]), []).append((m, i, j))
    table = np.full((DEVS, PER, DEVS, PER, CHOICES), -1, np.int32)
    for (a, b), places in found.items():
        for pa in range(PER):
            for pb in range(PER):
                ranked = {}
                for m, i, j in places:
                    ready = max(READY[i][pa], READY[j][pb])
                    ranked[m] = min(ranked.get(m, (9,)), (ready, i, j))
                codes = [((r * DEVS + m) << 8) | (i << 4) | j for r, m, i, j in sorted((r, m, i, j) for m, (r, i, j) in ranked.items())]
                codes = codes[:CHOICES]
                codes += codes[-1:] * (CHOICES - len(codes))
                table[a, pa, b, pb] = codes
    return table.reshape(-1)


HBM = pl.BlockSpec(memory_space=pltpu.HBM)
VM = pl.BlockSpec(memory_space=pltpu.VMEM)
SM = pl.BlockSpec(memory_space=pltpu.SMEM)
INFO = 2 + 2 * OVB


def params(mib=56):
    return pltpu.CompilerParams(vmem_limit_bytes=mib * 1024 * 1024)


def halves(a):
    high = a.astype(BF16)
    return high, (a - high.astype(F32)).astype(BF16)


def dot(a, b, ca=1, cb=0):
    return lax.dot_general(a, b, (((ca,), (cb,)), ((), ())), preferred_element_type=F32)


def dot3(a, b, cb=0):
    (ah, al), (bh, bl) = a, b
    return dot(ah, bh, 1, cb) + (dot(ah, bl, 1, cb) + dot(al, bh, 1, cb))


def newton_schulz(ref, count):
    for i in range(count):
        m = ref[i]
        total = jnp.sum(jnp.sum(m * m, axis=1, keepdims=True), axis=0, keepdims=True)
        ref[i] = m * lax.rsqrt(total + 1e-6)

    def step(_, carry):
        ms = [ref[i] for i in range(count)]
        hs = [halves(m) for m in ms]
        squares = [dot3(h, h, 1) for h in hs]
        sh = [halves(s) for s in squares]
        polys = [coef_second * s + coef_third * dot3(h, h) for s, h in zip(squares, sh)]
        ph = [halves(p) for p in polys]
        for i in range(count):
            ref[i] = coef_first * ms[i] + dot3(ph[i], hs[i])
        return carry

    lax.fori_loop(0, NS_STEPS, step, 0)


def index_kernel(me_ref, table_ref, ends_ref, blocks_ref, info_ref, count_ref, load_ref):
    me, base = me_ref[0], me_ref[1]
    for n in range((CLASSES + 1) * DEVS):
        load_ref[n] = 0

    def cost(code):
        place = code >> 8
        own = load_ref[place]
        late = jnp.where(place >= (CLASSES - 1) * DEVS, 2 * own + 4, 0)
        return own + late + load_ref[CLASSES * DEVS + (place & (DEVS - 1))]

    def step(q, carry):
        a, b = ends_ref[2 * q] - base, ends_ref[2 * q + 1] - base
        first = (a * (DEVS * PER) + b) * CHOICES
        code = table_ref[first]
        least = cost(code)
        for k in range(1, CHOICES):
            other = table_ref[first + k]
            less = cost(other)
            code = jnp.where(less < least, other, code)
            least = jnp.minimum(less, least)
        place = code >> 8
        device, ahead = place & (DEVS - 1), load_ref[place]
        load_ref[place] = ahead + 1
        load_ref[CLASSES * DEVS + device] += 1

        @pl.when(device == me)
        def _():
            line = ((place >> 5) * MAX_PAIRS + ahead) * INFO
            info_ref[line] = ((code >> 4) & 15) * PER + (a & 1)
            info_ref[line + 1] = (code & 15) * PER + (b & 1)
            for k in range(2 * OVB):
                info_ref[line + 2 + k] = blocks_ref[q * 2 * OVB + k]

        return carry

    lax.fori_loop(0, ends_ref.shape[0] // 2, step, 0)
    for c in range(CLASSES):
        count_ref[c] = load_ref[c * DEVS + me]


def make_index(me, table, ends, blocks):
    return pl.pallas_call(
        index_kernel,
        in_specs=[SM] * 4,
        out_specs=[SM] * 2,
        out_shape=[
            jax.ShapeDtypeStruct((CLASSES * MAX_PAIRS * INFO,), jnp.int32),
            jax.ShapeDtypeStruct((CLASSES,), jnp.int32),
        ],
        scratch_shapes=[pltpu.SMEM(((CLASSES + 1) * DEVS,), jnp.int32)],
        name="pair_index",
    )(me, table, ends, blocks)


def rotation_kernel(layout, ready, size, info_ref, count_ref, *refs):
    arrays, (rot_ref, rows, mats, outs, load_sem, out_sem) = refs[:-6], refs[-6:]
    count = count_ref[ready]
    first = jnp.int32(0)
    for c in range(ready):
        first = first + count_ref[c]
    batches = (count + size - 1) // size

    def block_ref(slot, block):
        number, part = layout[slot]
        ref = arrays[number]
        lines = pl.ds(pl.multiple_of(block * BLOCK, BLOCK), BLOCK)
        return ref.at[lines] if part is None else ref.at[part, lines]

    def load(batch, buf):
        def one(n, carry):
            i, e = n >> 1, n & 1
            line = (ready * MAX_PAIRS + jnp.minimum(batch * size + i, count - 1)) * INFO
            slot = info_ref[line + e]
            for s in layout:

                @pl.when(slot == s)
                def _():
                    for k in range(OVB):
                        pltpu.make_async_copy(
                            block_ref(s, info_ref[line + 2 + e * OVB + k]),
                            rows.at[buf, i, e, pl.ds(k * BLOCK, BLOCK)],
                            load_sem.at[buf],
                        ).start()

            return carry

        lax.fori_loop(0, 2 * size, one, 0)

    def out_copy(batch):
        return pltpu.make_async_copy(outs, rot_ref.at[pl.ds(first + batch * size, size)], out_sem)

    def work(batch):
        buf = batch & 1
        pltpu.make_async_copy(rows.at[buf], rows.at[buf], load_sem.at[buf]).wait()
        for i in range(size):
            mats[i] = dot(rows[buf, i, 1], rows[buf, i, 0], 0, 0)
        newton_schulz(mats, size)

        @pl.when(batch > 0)
        def _():
            out_copy(batch - 1).wait()

        for i in range(size):
            outs[i] = mats[i]
        out_copy(batch).start()

    def step(n, carry):
        @pl.when(n < batches)
        def _():
            load(n, n & 1)

        @pl.when(n > 0)
        def _():
            work(n - 1)

        return carry

    lax.fori_loop(0, batches + 1, step, 0)

    @pl.when(batches > 0)
    def _():
        out_copy(batches - 1).wait()


def make_rotations(info, count, arrays, layout, ready, size, rot=None):
    layout = {s: at for s, at in enumerate(layout) if at[0] < len(arrays)}
    more = [] if rot is None else [rot]
    return pl.pallas_call(
        functools.partial(rotation_kernel, layout, ready, size),
        in_specs=[SM, SM] + [HBM] * (len(arrays) + len(more)),
        out_specs=HBM,
        out_shape=jax.ShapeDtypeStruct((MAX_PAIRS + 8, D, D), F32),
        input_output_aliases={2 + len(arrays): 0} if more else {},
        scratch_shapes=[
            pltpu.VMEM((2, size, 2, OVB * BLOCK, D), BF16),
            pltpu.VMEM((size, D, D), F32),
            pltpu.VMEM((size, D, D), F32),
            pltpu.SemaphoreType.DMA((2,)),
            pltpu.SemaphoreType.DMA,
        ],
        compiler_params=params(60),
        name="rotations",
    )(info, count, *arrays, *more)


def start_kernel(start_ref, frame_ref, low_ref):
    for p in range(PER):
        frame_ref[p] = start_ref[p]
    newton_schulz(frame_ref, PER)
    low_ref[...] = frame_ref[...].astype(BF16)


def make_start(start):
    return pl.pallas_call(
        start_kernel,
        in_specs=[VM],
        out_specs=[VM, VM],
        out_shape=[
            jax.ShapeDtypeStruct((PER, D, D), F32),
            jax.ShapeDtypeStruct((PER, D, D), BF16),
        ],
        compiler_params=params(),
        name="start_frames",
    )(start)


def estimate_kernel(info_ref, count_ref, rot_ref, *refs):
    lows = refs[:SLOTS]
    outs = refs[SLOTS : SLOTS + OWN + 1]
    frames, acc, rot, frame_sem, rot_sem, out_sem = refs[SLOTS + OWN + 1 :]
    ends = [count_ref[0]]
    for c in range(1, CLASSES):
        ends.append(ends[-1] + count_ref[c])
    count = ends[-1]

    def line_of(j):
        line = j
        for c in range(1, CLASSES):
            line = jnp.where(j >= ends[c - 1], c * MAX_PAIRS + j - ends[c - 1], line)
        return line * INFO

    def rot_copy(t, buf):
        return pltpu.make_async_copy(rot_ref.at[pl.ds(2 * t, 2)], rot.at[buf], rot_sem.at[buf])

    copies = [
        pltpu.make_async_copy(lows[s], frames.at[pl.ds(s * PER, PER)], frame_sem.at[s])
        for s in range(SLOTS)
    ]
    for copy in copies:
        copy.start()

    @pl.when(count > 0)
    def _():
        rot_copy(0, 0).start()

    acc[...] = jnp.zeros_like(acc)
    for copy in copies:
        copy.wait()

    def step(t, carry):
        buf = t & 1

        @pl.when(2 * t + 2 < count)
        def _():
            rot_copy(t + 1, 1 - buf).start()

        rot_copy(t, buf).wait()
        found = []
        for i in range(2):
            line = line_of(jnp.minimum(2 * t + i, count - 1))
            sa, sb = info_ref[line], info_ref[line + 1]
            high, rest = halves(rot[buf, i])
            fa, fb = frames[sa], frames[sb]
            found.append((sa, dot(high, fb, 0, 0) + dot(rest, fb, 0, 0), sb, dot(high, fa) + dot(rest, fa)))

        def add(sa, ea, sb, eb):
            acc[sa] += ea
            acc[sb] += eb

        add(*found[0])

        @pl.when(2 * t + 1 < count)
        def _():
            add(*found[1])

        return carry

    lax.fori_loop(0, (count + 1) // 2, step, 0)
    parts = [(s * PER, PER) for s in range(OWN)] + [(OWN * PER, len(CROSS) * PER)]
    copies = [
        pltpu.make_async_copy(acc.at[pl.ds(*part)], outs[n], out_sem.at[n]) for n, part in enumerate(parts)
    ]
    for copy in copies:
        copy.start()
    for copy in copies:
        copy.wait()


def make_estimates(info, count, rot, lows):
    return pl.pallas_call(
        estimate_kernel,
        in_specs=[SM, SM, HBM] + [HBM] * SLOTS,
        out_specs=[HBM] * (OWN + 1),
        out_shape=[jax.ShapeDtypeStruct((PER, D, D), F32)] * OWN
        + [jax.ShapeDtypeStruct((len(CROSS) * PER, D, D), F32)],
        scratch_shapes=[
            pltpu.VMEM((SLOTS * PER, D, D), BF16),
            pltpu.VMEM((SLOTS * PER, D, D), F32),
            pltpu.VMEM((2, 2, D, D), F32),
            pltpu.SemaphoreType.DMA((SLOTS,)),
            pltpu.SemaphoreType.DMA((2,)),
            pltpu.SemaphoreType.DMA((OWN + 1,)),
        ],
        compiler_params=params(),
        name="estimates",
    )(info, count, rot, *lows)


def update_kernel(core_ref, frame_ref, *refs):
    parts, (out_ref, *more) = refs[: OWN - 2], refs[OWN - 2 :]
    for p in range(PER):
        total = frame_ref[p]
        for part in parts:
            total = total + part[p]
        out_ref[p] = total
    newton_schulz(out_ref, PER)
    if len(more) == 1:
        more[0][...] = out_ref[...].astype(BF16)
    else:
        for ref, half in zip(more, (core_ref[0], 1 - core_ref[0])):
            rows = pl.ds(pl.multiple_of(half * (D // 2), D // 2), D // 2)
            ref[...] = out_ref[0, rows] + out_ref[1, rows]


def make_update(frames, parts, core=None):
    more = [jax.ShapeDtypeStruct((PER, D, D), BF16)]
    if core is not None:
        more = [jax.ShapeDtypeStruct((D // 2, D), F32)] * 2
    return pl.pallas_call(
        update_kernel,
        in_specs=[SM] + [VM] * (1 + len(parts)),
        out_specs=[VM] * (1 + len(more)),
        out_shape=[jax.ShapeDtypeStruct((PER, D, D), F32)] + more,
        compiler_params=params(),
        name="update_frames",
    )(jnp.zeros(1, jnp.int32) if core is None else core, frames, *parts)


CHUNK = 512


def final_kernel(
    core_ref, keep_ref, other_ref, frame_ref, patch_ref, aligned_ref, final_ref, total_ref, gauge, rows, outs, low, in_sem, out_sem
):
    pieces = patch_ref.shape[1] // CHUNK

    def lines(n):
        return pl.ds(pl.multiple_of(n * CHUNK, CHUNK), CHUNK)

    def copy_in(p, n):
        return pltpu.make_async_copy(patch_ref.at[p, lines(n)], rows.at[p, lines(n)], in_sem.at[p, n])

    def copy_out(p, n):
        return pltpu.make_async_copy(outs.at[p, lines(n)], aligned_ref.at[p, lines(n)], out_sem.at[p, n])

    every = [(p, n) for n in range(pieces) for p in range(PER)]
    for at in every:
        copy_in(*at).start()
    for ref, half in ((keep_ref, core_ref[0]), (other_ref, 1 - core_ref[0])):
        total_ref[pl.ds(pl.multiple_of(half * (D // 2), D // 2), D // 2)] = ref[...]
    gauge[0] = total_ref[...]
    newton_schulz(gauge, 1)
    g = halves(gauge[0])
    for p in range(PER):
        final = dot3(halves(frame_ref[p]), g, 1)
        final_ref[p] = final
        low[p] = final.astype(BF16)

    def step(n, carry):
        for p in range(PER):
            copy_in(p, n).wait()
        found = [dot(rows[p, lines(n)], low[p]).astype(BF16) for p in range(PER)]
        for p in range(PER):
            outs[p, lines(n)] = found[p]
            copy_out(p, n).start()
        return carry

    lax.fori_loop(0, pieces, step, 0)
    for at in every:
        copy_out(*at).wait()


def make_final(core, keep, other, frames, patches):
    pieces = patches.shape[1] // CHUNK
    return pl.pallas_call(
        final_kernel,
        in_specs=[SM, VM, VM, VM, HBM],
        out_specs=[HBM, VM, VM],
        out_shape=[
            jax.ShapeDtypeStruct(patches.shape, BF16),
            jax.ShapeDtypeStruct((PER, D, D), F32),
            jax.ShapeDtypeStruct((D, D), F32),
        ],
        scratch_shapes=[
            pltpu.VMEM((1, D, D), F32),
            pltpu.VMEM(patches.shape, BF16),
            pltpu.VMEM(patches.shape, BF16),
            pltpu.VMEM((PER, D, D), BF16),
            pltpu.SemaphoreType.DMA((PER, pieces)),
            pltpu.SemaphoreType.DMA((PER, pieces)),
        ],
        compiler_params=params(),
        name="aligned_rows",
    )(core, keep, other, frames, patches)


def send(value, perm):
    return lax.ppermute(value, GY, perm)


LAYOUT = ((0, 0), (0, 1)) + tuple(
    (n, None) for n in (1, 2, 13, 7, 10, 14, 3, 4, 8, 9, 5, 6, 15, 11, 12, 16)
)


def back_perm(steps):
    return [(d, m) for m, d in step_perm(steps)]


def spread_frames(low):
    one, four = send(low, step_perm(UP)), send(low, step_perm(LEFT))
    three = send(low, step_perm(RIGHT))
    two, five = send(one, step_perm(UP)), send(four, step_perm(LEFT))
    return [low, one, two, three, four, five] + [send(v, SIBLING) for v in (one, two, three)]


def bring_back(parts):
    own, one, two, three, four, five, cross = parts
    cross = send(cross, SIBLING)
    five = send(five, back_perm(LEFT))
    one, two, three = (
        lax.optimization_barrier(v + cross[PER * n : PER * (n + 1)]) for n, v in enumerate((one, two, three))
    )
    two = send(two, back_perm(UP))
    three = send(three, back_perm(RIGHT))
    four = send(four + five, back_perm(LEFT))
    return [own, three, four, send(one + two, back_perm(UP))]


def axis_sum(value, axis):
    size = lax.axis_size(axis)

    def from_behind(hops):
        return lax.ppermute(value, axis, [(i, (i + hops) % size) for i in range(size)])

    near = from_behind(1), from_behind(-1)
    return (value + near[0]) + (near[1] + from_behind(2))


def sum_over_all(keep, give):
    swap = [(0, 1), (1, 0)]
    keep = keep + lax.ppermute(give, "gy_2", swap)
    for axis in ("gx", "gy_0", "gy_1"):
        keep = axis_sum(keep, axis)
    return keep, lax.ppermute(keep, "gy_2", swap)


def local(patches, start_frames, pair_ends, margin_blocks):
    me = lax.axis_index(GY).astype(jnp.int32)
    base = lax.axis_index("gx").astype(jnp.int32) * (DEVS * PER)

    def move(value, steps=None):
        return send(value, step_perm(steps) if steps else SIBLING)

    upper = patches[1]
    four_1, one_1 = move(upper, LEFT), move(upper, UP)
    lower = lax.optimization_barrier(patches)[0]
    four_0, one_0 = move(lower, LEFT), move(lower, UP)
    info, count = make_index(
        jnp.stack([me, base]),
        jnp.asarray(meeting_table()),
        pair_ends.reshape(-1),
        margin_blocks.reshape(-1),
    )
    frames, low = make_start(start_frames)
    lows = spread_frames(low)
    five_1, two_1 = move(four_1, LEFT), move(one_1, UP)
    five_0, two_0 = move(four_0, LEFT), move(one_0, UP)
    three_0 = move(lower, RIGHT)
    arrays = [patches, one_0, one_1, four_0, four_1, move(one_0), move(one_1)]
    rot = make_rotations(info, count, arrays, LAYOUT, 0, 3)
    three_1 = move(five_1, LEFT)
    arrays += [two_1, five_0, five_1, three_0, move(two_1), move(three_0)]
    rot = make_rotations(info, count, arrays, LAYOUT, 1, 7, rot)
    arrays += [two_0, three_1, move(two_0), move(three_1)]
    rot = make_rotations(info, count, arrays, LAYOUT, 2, 5, rot)
    core = lax.axis_index("gy_2").astype(jnp.int32).reshape(1)
    for sweep in range(SWEEPS):
        if sweep:
            lows = spread_frames(low)
        back = bring_back(make_estimates(info, count, rot, lows))
        if sweep < SWEEPS - 1:
            frames, low = make_update(frames, back)
        else:
            frames, keep, give = make_update(frames, back, core)
    keep, other = sum_over_all(keep, give)
    aligned, final_frames, total = make_final(core, keep, other, frames, patches)
    return aligned, final_frames, total


def solution(mesh):
    torus = Mesh(mesh.devices.reshape(mesh.shape["gx"], 4, 4, 2), ("gx", "gy_0", "gy_1", "gy_2"))
    return jax.shard_map(
        local,
        mesh=torus,
        in_specs=(P(GX_GY, None, None), P(GX_GY, None, None), P("gx", None), P("gx", None, None)),
        out_specs=(P(GX_GY, None, None), P(GX_GY, None, None), P()),
        check_vma=False,
    )
```

```python
import functools

import jax
import jax.numpy as jnp
import numpy as np
from jax import lax
from jax.experimental import pallas as pl
from jax.experimental.pallas import tpu as pltpu
from jax.sharding import Mesh
from jax.sharding import PartitionSpec as P


BLOCK = 128
OVB = 4
D = 256
SWEEPS = 2
NS_STEPS = 5
PER = 2
DEVS = 32
GY = ("gy_0", "gy_1", "gy_2")
GX_GY = ("gx", "gy_0", "gy_1", "gy_2")
F32, BF16 = jnp.float32, jnp.bfloat16

coef_first = 3.4445
coef_second = -4.775
coef_third = 2.0315

OFFS = (
    ((0, 0), (1, 0), (2, 0), (0, 1), (0, 3), (0, 2)),
    ((0, 0), (0, 1), (0, 2), (1, 0), (3, 0), (2, 0)),
)
CROSS = (1, 2, 3)
OWN = len(OFFS[0])
SLOTS = OWN + len(CROSS)
MAX_PAIRS = SLOTS * DEVS // 2


def device_at(z, x, c):
    return (z % 4) * 8 + (x % 4) * 2 + c % 2


def place_of(m):
    return m // 8, (m // 2) % 4, m % 2


def step_perm(steps):
    perm = []
    for m in range(DEVS):
        z, x, c = place_of(m)
        dz, dx = steps[c]
        perm.append((m, device_at(z + dz, x + dx, c)))
    return perm


def flip(step):
    return (step, (step[1], step[0]))


UP, RIGHT, LEFT = flip((1, 0)), flip((0, 1)), flip((0, -1))
SIBLING = [(m, m ^ 1) for m in range(DEVS)]


@functools.cache
def sources():
    same = []
    for m in range(DEVS):
        z, x, c = place_of(m)
        same.append([device_at(z - dz, x - dx, c) for dz, dx in OFFS[c]])
    return [same[m] + [same[m ^ 1][k] for k in CROSS] for m in range(DEVS)]


READY = ((0, 0), (0, 0), (2, 1), (1, 2), (0, 0), (1, 1), (0, 0), (2, 1), (1, 2))
CLASSES = 3
CHOICES = 3


@functools.cache
def meeting_table():
    found = {}
    src = sources()
    for m in range(DEVS):
        for i in range(SLOTS):
            for j in range(SLOTS):
                if src[m][i] != src[m][j]:
                    found.setdefault((src[m][i], src[m][j]), []).append((m, i, j))
    table = np.full((DEVS, PER, DEVS, PER, CHOICES), -1, np.int32)
    for (a, b), places in found.items():
        for pa in range(PER):
            for pb in range(PER):
                ranked = {}
                for m, i, j in places:
                    ready = max(READY[i][pa], READY[j][pb])
                    ranked[m] = min(ranked.get(m, (9,)), (ready, i, j))
                codes = [((r * DEVS + m) << 8) | (i << 4) | j for r, m, i, j in sorted((r, m, i, j) for m, (r, i, j) in ranked.items())]
                codes = codes[:CHOICES]
                codes += codes[-1:] * (CHOICES - len(codes))
                table[a, pa, b, pb] = codes
    return table.reshape(-1)


HBM = pl.BlockSpec(memory_space=pltpu.HBM)
VM = pl.BlockSpec(memory_space=pltpu.VMEM)
SM = pl.BlockSpec(memory_space=pltpu.SMEM)
INFO = 2 + 2 * OVB


def params(mib=56):
    return pltpu.CompilerParams(vmem_limit_bytes=mib * 1024 * 1024)


def halves(a):
    high = a.astype(BF16)
    return high, (a - high.astype(F32)).astype(BF16)


def dot(a, b, ca=1, cb=0):
    return lax.dot_general(a, b, (((ca,), (cb,)), ((), ())), preferred_element_type=F32)


def dot3(a, b, cb=0):
    (ah, al), (bh, bl) = a, b
    return dot(ah, bh, 1, cb) + (dot(ah, bl, 1, cb) + dot(al, bh, 1, cb))


def newton_schulz(ref, count):
    for i in range(count):
        m = ref[i]
        total = jnp.sum(jnp.sum(m * m, axis=1, keepdims=True), axis=0, keepdims=True)
        ref[i] = m * lax.rsqrt(total + 1e-6)

    def step(_, carry):
        ms = [ref[i] for i in range(count)]
        hs = [halves(m) for m in ms]
        squares = [dot3(h, h, 1) for h in hs]
        sh = [halves(s) for s in squares]
        polys = [coef_second * s + coef_third * dot3(h, h) for s, h in zip(squares, sh)]
        ph = [halves(p) for p in polys]
        for i in range(count):
            ref[i] = coef_first * ms[i] + dot3(ph[i], hs[i])
        return carry

    lax.fori_loop(0, NS_STEPS, step, 0)


def index_kernel(me_ref, table_ref, ends_ref, blocks_ref, info_ref, count_ref, load_ref):
    me, base = me_ref[0], me_ref[1]
    for n in range((CLASSES + 1) * DEVS):
        load_ref[n] = 0

    def cost(code):
        place = code >> 8
        own = load_ref[place]
        late = jnp.where(place >= (CLASSES - 1) * DEVS, 2 * own + 4, 0)
        return own + late + load_ref[CLASSES * DEVS + (place & (DEVS - 1))]

    def step(q, carry):
        a, b = ends_ref[2 * q] - base, ends_ref[2 * q + 1] - base
        first = (a * (DEVS * PER) + b) * CHOICES
        code = table_ref[first]
        least = cost(code)
        for k in range(1, CHOICES):
            other = table_ref[first + k]
            less = cost(other)
            code = jnp.where(less < least, other, code)
            least = jnp.minimum(less, least)
        place = code >> 8
        device, ahead = place & (DEVS - 1), load_ref[place]
        load_ref[place] = ahead + 1
        load_ref[CLASSES * DEVS + device] += 1

        @pl.when(device == me)
        def _():
            line = ((place >> 5) * MAX_PAIRS + ahead) * INFO
            info_ref[line] = ((code >> 4) & 15) * PER + (a & 1)
            info_ref[line + 1] = (code & 15) * PER + (b & 1)
            for k in range(2 * OVB):
                info_ref[line + 2 + k] = blocks_ref[q * 2 * OVB + k]

        return carry

    lax.fori_loop(0, ends_ref.shape[0] // 2, step, 0)
    for c in range(CLASSES):
        count_ref[c] = load_ref[c * DEVS + me]


def make_index(me, table, ends, blocks):
    return pl.pallas_call(
        index_kernel,
        in_specs=[SM] * 4,
        out_specs=[SM] * 2,
        out_shape=[
            jax.ShapeDtypeStruct((CLASSES * MAX_PAIRS * INFO,), jnp.int32),
            jax.ShapeDtypeStruct((CLASSES,), jnp.int32),
        ],
        scratch_shapes=[pltpu.SMEM(((CLASSES + 1) * DEVS,), jnp.int32)],
        name="pair_index",
    )(me, table, ends, blocks)


def rotation_kernel(layout, ready, size, info_ref, count_ref, *refs):
    arrays, (rot_ref, rows, mats, outs, load_sem, out_sem) = refs[:-6], refs[-6:]
    count = count_ref[ready]
    first = jnp.int32(0)
    for c in range(ready):
        first = first + count_ref[c]
    batches = (count + size - 1) // size

    def block_ref(slot, block):
        number, part = layout[slot]
        ref = arrays[number]
        lines = pl.ds(pl.multiple_of(block * BLOCK, BLOCK), BLOCK)
        return ref.at[lines] if part is None else ref.at[part, lines]

    def load(batch, buf):
        def one(n, carry):
            i, e = n >> 1, n & 1
            line = (ready * MAX_PAIRS + jnp.minimum(batch * size + i, count - 1)) * INFO
            slot = info_ref[line + e]
            for s in layout:

                @pl.when(slot == s)
                def _():
                    for k in range(OVB):
                        pltpu.make_async_copy(
                            block_ref(s, info_ref[line + 2 + e * OVB + k]),
                            rows.at[buf, i, e, pl.ds(k * BLOCK, BLOCK)],
                            load_sem.at[buf],
                        ).start()

            return carry

        lax.fori_loop(0, 2 * size, one, 0)

    def out_copy(batch):
        return pltpu.make_async_copy(outs, rot_ref.at[pl.ds(first + batch * size, size)], out_sem)

    def work(batch):
        buf = batch & 1
        pltpu.make_async_copy(rows.at[buf], rows.at[buf], load_sem.at[buf]).wait()
        for i in range(size):
            mats[i] = dot(rows[buf, i, 1], rows[buf, i, 0], 0, 0)
        newton_schulz(mats, size)

        @pl.when(batch > 0)
        def _():
            out_copy(batch - 1).wait()

        for i in range(size):
            outs[i] = mats[i]
        out_copy(batch).start()

    def step(n, carry):
        @pl.when(n < batches)
        def _():
            load(n, n & 1)

        @pl.when(n > 0)
        def _():
            work(n - 1)

        return carry

    lax.fori_loop(0, batches + 1, step, 0)

    @pl.when(batches > 0)
    def _():
        out_copy(batches - 1).wait()


def make_rotations(info, count, arrays, layout, ready, size, rot=None):
    layout = {s: at for s, at in enumerate(layout) if at[0] < len(arrays)}
    more = [] if rot is None else [rot]
    return pl.pallas_call(
        functools.partial(rotation_kernel, layout, ready, size),
        in_specs=[SM, SM] + [HBM] * (len(arrays) + len(more)),
        out_specs=HBM,
        out_shape=jax.ShapeDtypeStruct((MAX_PAIRS + 8, D, D), F32),
        input_output_aliases={2 + len(arrays): 0} if more else {},
        scratch_shapes=[
            pltpu.VMEM((2, size, 2, OVB * BLOCK, D), BF16),
            pltpu.VMEM((size, D, D), F32),
            pltpu.VMEM((size, D, D), F32),
            pltpu.SemaphoreType.DMA((2,)),
            pltpu.SemaphoreType.DMA,
        ],
        compiler_params=params(60),
        name="rotations",
    )(info, count, *arrays, *more)


def start_kernel(start_ref, frame_ref, low_ref):
    for p in range(PER):
        frame_ref[p] = start_ref[p]
    newton_schulz(frame_ref, PER)
    low_ref[...] = frame_ref[...].astype(BF16)


def make_start(start):
    return pl.pallas_call(
        start_kernel,
        in_specs=[VM],
        out_specs=[VM, VM],
        out_shape=[
            jax.ShapeDtypeStruct((PER, D, D), F32),
            jax.ShapeDtypeStruct((PER, D, D), BF16),
        ],
        compiler_params=params(),
        name="start_frames",
    )(start)


def estimate_kernel(info_ref, count_ref, rot_ref, *refs):
    lows = refs[:SLOTS]
    outs = refs[SLOTS : SLOTS + OWN + 1]
    frames, acc, rot, frame_sem, rot_sem, out_sem = refs[SLOTS + OWN + 1 :]
    ends = [count_ref[0]]
    for c in range(1, CLASSES):
        ends.append(ends[-1] + count_ref[c])
    count = ends[-1]

    def line_of(j):
        line = j
        for c in range(1, CLASSES):
            line = jnp.where(j >= ends[c - 1], c * MAX_PAIRS + j - ends[c - 1], line)
        return line * INFO

    def rot_copy(t, buf):
        return pltpu.make_async_copy(rot_ref.at[pl.ds(2 * t, 2)], rot.at[buf], rot_sem.at[buf])

    copies = [
        pltpu.make_async_copy(lows[s], frames.at[pl.ds(s * PER, PER)], frame_sem.at[s])
        for s in range(SLOTS)
    ]
    for copy in copies:
        copy.start()

    @pl.when(count > 0)
    def _():
        rot_copy(0, 0).start()

    acc[...] = jnp.zeros_like(acc)
    for copy in copies:
        copy.wait()

    def step(t, carry):
        buf = t & 1

        @pl.when(2 * t + 2 < count)
        def _():
            rot_copy(t + 1, 1 - buf).start()

        rot_copy(t, buf).wait()
        found = []
        for i in range(2):
            line = line_of(jnp.minimum(2 * t + i, count - 1))
            sa, sb = info_ref[line], info_ref[line + 1]
            high, rest = halves(rot[buf, i])
            fa, fb = frames[sa], frames[sb]
            found.append((sa, dot(high, fb, 0, 0) + dot(rest, fb, 0, 0), sb, dot(high, fa) + dot(rest, fa)))

        def add(sa, ea, sb, eb):
            acc[sa] += ea
            acc[sb] += eb

        add(*found[0])

        @pl.when(2 * t + 1 < count)
        def _():
            add(*found[1])

        return carry

    lax.fori_loop(0, (count + 1) // 2, step, 0)
    parts = [(s * PER, PER) for s in range(OWN)] + [(OWN * PER, len(CROSS) * PER)]
    copies = [
        pltpu.make_async_copy(acc.at[pl.ds(*part)], outs[n], out_sem.at[n]) for n, part in enumerate(parts)
    ]
    for copy in copies:
        copy.start()
    for copy in copies:
        copy.wait()


def make_estimates(info, count, rot, lows):
    return pl.pallas_call(
        estimate_kernel,
        in_specs=[SM, SM, HBM] + [HBM] * SLOTS,
        out_specs=[HBM] * (OWN + 1),
        out_shape=[jax.ShapeDtypeStruct((PER, D, D), F32)] * OWN
        + [jax.ShapeDtypeStruct((len(CROSS) * PER, D, D), F32)],
        scratch_shapes=[
            pltpu.VMEM((SLOTS * PER, D, D), BF16),
            pltpu.VMEM((SLOTS * PER, D, D), F32),
            pltpu.VMEM((2, 2, D, D), F32),
            pltpu.SemaphoreType.DMA((SLOTS,)),
            pltpu.SemaphoreType.DMA((2,)),
            pltpu.SemaphoreType.DMA((OWN + 1,)),
        ],
        compiler_params=params(),
        name="estimates",
    )(info, count, rot, *lows)


def update_kernel(core_ref, frame_ref, *refs):
    parts, (out_ref, *more) = refs[: OWN - 2], refs[OWN - 2 :]
    for p in range(PER):
        total = frame_ref[p]
        for part in parts:
            total = total + part[p]
        out_ref[p] = total
    newton_schulz(out_ref, PER)
    if len(more) == 1:
        more[0][...] = out_ref[...].astype(BF16)
    else:
        for ref, half in zip(more, (core_ref[0], 1 - core_ref[0])):
            rows = pl.ds(pl.multiple_of(half * (D // 2), D // 2), D // 2)
            ref[...] = out_ref[0, rows] + out_ref[1, rows]


def make_update(frames, parts, core=None):
    more = [jax.ShapeDtypeStruct((PER, D, D), BF16)]
    if core is not None:
        more = [jax.ShapeDtypeStruct((D // 2, D), F32)] * 2
    return pl.pallas_call(
        update_kernel,
        in_specs=[SM] + [VM] * (1 + len(parts)),
        out_specs=[VM] * (1 + len(more)),
        out_shape=[jax.ShapeDtypeStruct((PER, D, D), F32)] + more,
        compiler_params=params(),
        name="update_frames",
    )(jnp.zeros(1, jnp.int32) if core is None else core, frames, *parts)


CHUNK = 1024


def final_kernel(
    core_ref, keep_ref, other_ref, frame_ref, patch_ref, aligned_ref, final_ref, total_ref, gauge, rows, outs, low, in_sem, out_sem
):
    pieces = patch_ref.shape[1] // CHUNK

    def piece(n):
        return n // pieces, pl.ds(pl.multiple_of(n % pieces * CHUNK, CHUNK), CHUNK)

    def copy_in(n):
        p, r = piece(n)
        return pltpu.make_async_copy(patch_ref.at[p, r], rows.at[p, r], in_sem.at[n])

    def copy_out(n):
        p, r = piece(n)
        return pltpu.make_async_copy(outs.at[p, r], aligned_ref.at[p, r], out_sem.at[n])

    for n in range(PER * pieces):
        copy_in(n).start()
    for ref, half in ((keep_ref, core_ref[0]), (other_ref, 1 - core_ref[0])):
        total_ref[pl.ds(pl.multiple_of(half * (D // 2), D // 2), D // 2)] = ref[...]
    gauge[0] = total_ref[...]
    newton_schulz(gauge, 1)
    g = halves(gauge[0])
    for p in range(PER):
        final = dot3(halves(frame_ref[p]), g, 1)
        final_ref[p] = final
        low[p] = final.astype(BF16)

    def step(n, carry):
        p, r = piece(n)
        copy_in(n).wait()
        outs[p, r] = dot(rows[p, r], low[p]).astype(BF16)
        copy_out(n).start()
        return carry

    lax.fori_loop(0, PER * pieces, step, 0)
    for n in range(PER * pieces):
        copy_out(n).wait()


def make_final(core, keep, other, frames, patches):
    pieces = PER * patches.shape[1] // CHUNK
    return pl.pallas_call(
        final_kernel,
        in_specs=[SM, VM, VM, VM, HBM],
        out_specs=[HBM, VM, VM],
        out_shape=[
            jax.ShapeDtypeStruct(patches.shape, BF16),
            jax.ShapeDtypeStruct((PER, D, D), F32),
            jax.ShapeDtypeStruct((D, D), F32),
        ],
        scratch_shapes=[
            pltpu.VMEM((1, D, D), F32),
            pltpu.VMEM(patches.shape, BF16),
            pltpu.VMEM(patches.shape, BF16),
            pltpu.VMEM((PER, D, D), BF16),
            pltpu.SemaphoreType.DMA((pieces,)),
            pltpu.SemaphoreType.DMA((pieces,)),
        ],
        compiler_params=params(),
        name="aligned_rows",
    )(core, keep, other, frames, patches)


def send(value, perm):
    return lax.ppermute(value, GY, perm)


LAYOUT = ((0, 0), (0, 1)) + tuple(
    (n, None) for n in (1, 2, 13, 7, 10, 14, 3, 4, 8, 9, 5, 6, 15, 11, 12, 16)
)


def back_perm(steps):
    return [(d, m) for m, d in step_perm(steps)]


def spread_frames(low):
    one, four, three = send(low, step_perm(UP)), send(low, step_perm(LEFT)), send(low, step_perm(RIGHT))
    two, five = send(one, step_perm(UP)), send(four, step_perm(LEFT))
    return [low, one, two, three, four, five] + [send(v, SIBLING) for v in (one, two, three)]


def bring_back(parts):
    own, one, two, three, four, five, cross = parts
    cross = send(cross, SIBLING)
    five = send(five, back_perm(LEFT))
    one, two, three = (
        lax.optimization_barrier(v + cross[PER * n : PER * (n + 1)]) for n, v in enumerate((one, two, three))
    )
    two = send(two, back_perm(UP))
    three = send(three, back_perm(RIGHT))
    return [own, three, send(four + five, back_perm(LEFT)), send(one + two, back_perm(UP))]


def axis_sum(value, axis):
    size = lax.axis_size(axis)

    def from_behind(hops):
        return lax.ppermute(value, axis, [(i, (i + hops) % size) for i in range(size)])

    near = from_behind(1), from_behind(-1)
    return (value + near[0]) + (near[1] + from_behind(2))


def sum_over_all(keep, give):
    swap = [(0, 1), (1, 0)]
    keep = keep + lax.ppermute(give, "gy_2", swap)
    for axis in ("gx", "gy_0", "gy_1"):
        keep = axis_sum(keep, axis)
    return keep, lax.ppermute(keep, "gy_2", swap)


def local(patches, start_frames, pair_ends, margin_blocks):
    me = lax.axis_index(GY).astype(jnp.int32)
    base = lax.axis_index("gx").astype(jnp.int32) * (DEVS * PER)

    def move(value, steps=None):
        return send(value, step_perm(steps) if steps else SIBLING)

    upper = patches[1]
    four_1, one_1 = move(upper, LEFT), move(upper, UP)
    lower = lax.optimization_barrier(patches)[0]
    four_0, one_0 = move(lower, LEFT), move(lower, UP)
    info, count = make_index(
        jnp.stack([me, base]),
        jnp.asarray(meeting_table()),
        pair_ends.reshape(-1),
        margin_blocks.reshape(-1),
    )
    frames, low = make_start(start_frames)
    lows = spread_frames(low)
    five_1, two_1 = move(four_1, LEFT), move(one_1, UP)
    five_0, two_0 = move(four_0, LEFT), move(one_0, UP)
    three_0 = move(lower, RIGHT)
    arrays = [patches, one_0, one_1, four_0, four_1, move(one_0), move(one_1)]
    rot = make_rotations(info, count, arrays, LAYOUT, 0, 3)
    three_1 = move(five_1, LEFT)
    arrays += [two_1, five_0, five_1, three_0, move(two_1), move(three_0)]
    rot = make_rotations(info, count, arrays, LAYOUT, 1, 4, rot)
    arrays += [two_0, three_1, move(two_0), move(three_1)]
    rot = make_rotations(info, count, arrays, LAYOUT, 2, 5, rot)
    core = lax.axis_index("gy_2").astype(jnp.int32).reshape(1)
    for sweep in range(SWEEPS):
        if sweep:
            lows = spread_frames(low)
        back = bring_back(make_estimates(info, count, rot, lows))
        if sweep < SWEEPS - 1:
            frames, low = make_update(frames, back)
        else:
            frames, keep, give = make_update(frames, back, core)
    keep, other = sum_over_all(keep, give)
    aligned, final_frames, total = make_final(core, keep, other, frames, patches)
    return aligned, final_frames, total


def solution(mesh):
    torus = Mesh(mesh.devices.reshape(mesh.shape["gx"], 4, 4, 2), ("gx", "gy_0", "gy_1", "gy_2"))
    return jax.shard_map(
        local,
        mesh=torus,
        in_specs=(P(GX_GY, None, None), P(GX_GY, None, None), P("gx", None), P("gx", None, None)),
        out_specs=(P(GX_GY, None, None), P(GX_GY, None, None), P()),
        check_vma=False,
    )
```
